768 devices in a mesh: gx: 16 (over y, core), gy: 12 (over x, z_hi), gz: 4 (over z_lo).
Axes of the slice: x: 4, y: 8, z: 12 (z_hi: 3, z_lo: 4; z = z_hi * 4 + z_lo), core: 2. Of those that a mesh axis runs over, the one named last changes fastest.
Arguments:
- panels: bfloat16 [4, 4, 16, 96, 8192], P(None, None, 'gz', 'gy', 'gx'), may hold values from -6 to 6
- eof_basis: bfloat16 [4, 16, 10], replicated, may hold values from -1.5 to 1.5
- control: float32 [4, 10, 96, 8192], P(None, None, 'gy', ('gx', 'gz')), may hold values from -6 to 6
- coefficients: float32 [4, 96, 8192], P(None, 'gy', ('gx', 'gz')), may hold values from -0.5 to 1.6, as said below
Outputs:
- covariance_image: float32 [4, 10, 96, 8192], P(None, None, 'gy', ('gx', 'gz'))
The draws below stay inside these ranges and needn't reach their ends.
Inputs may be any that keep to these rules, and one draw needn't show every extreme that they name: `coefficients`: kxx and kyy lie in 0.2 to 1, kxy = c sqrt(kxx kyy) with c in -0.5 to 0.5, and the inverse cell area lies in 0.6 to 1.6.
All inputs are finite; a program needn't handle non-finite values.
Results may differ from the reference program's by a relative error of at most 0.00085.
Values may be sent and summed in bfloat16 or wider, within the bound.
A program may use at most 32 MiB of HBM per device.

```python
import jax
import jax.numpy as jnp
from jax import lax

F = 4
EOF = 10
M = 4
LEV = 16
STEPS = 6
NX = 8192
NY = 96


def draw_coefficients(key, part):
    keys = jax.random.split(key, 4)
    east_coeff = jax.random.uniform(keys[0], (NY, NX), jnp.float32, 0.2, 1.0)
    north_coeff = jax.random.uniform(keys[1], (NY, NX), jnp.float32, 0.2, 1.0)
    tilt = jax.random.uniform(keys[2], (NY, NX), jnp.float32, -0.5, 0.5)
    area_inv = jax.random.uniform(keys[3], (NY, NX), jnp.float32, 0.6, 1.6)
    cross = tilt * jnp.sqrt(east_coeff * north_coeff)
    return jnp.stack([east_coeff, cross, north_coeff, area_inv], axis=0)


def block_levels(rng, extent, pieces, low, high):
    def one(dim, shards_of):
        steps = jax.random.uniform(jax.random.fold_in(jax.random.fold_in(rng, 6), dim), (shards_of,), jnp.float32, low / len(pieces), high / len(pieces))
        return jnp.repeat(jnp.exp(steps), extent[dim] // shards_of).reshape((-1,) + (1,) * (len(extent) - dim - 1))

    loudness = one(*pieces[0])
    for cut in pieces[1:]:
        loudness = loudness * one(*cut)
    return loudness


def bell_draw(rng, extent, width, reach, pieces=(), dtype=jnp.bfloat16):
    entries = jax.random.normal(rng, extent, jnp.float32) * width
    if len(pieces) > 0:
        entries = block_levels(rng, extent, pieces, -0.22, 0.18) * entries
    return jnp.clip(entries, min=-reach, max=reach).astype(dtype)


def setup_inputs(seed: int = 0) -> dict:
    streams_of = jax.random.split(jax.random.key(seed), 5)
    panels = bell_draw(streams_of[0], (M, F, LEV, NY, NX), 1.0, 6.0, ((2, 4), (3, 12), (4, 16)))
    eof_basis = bell_draw(streams_of[1], (F, LEV, EOF), LEV ** -0.5, 1.5)
    control = bell_draw(streams_of[2], (F, EOF, NY, NX), 1.0, 6.0, ((2, 12), (3, 64)), jnp.float32)
    coefficients = draw_coefficients(jax.random.fold_in(streams_of[4], 71), 0)
    return dict(panels=panels, eof_basis=eof_basis, control=control, coefficients=coefficients)


time_step = 0.09

def divergence(padded, coeffs):
    east_diff = padded[:, :-1, 1:] - padded[:, :-1, :-1]
    north_diff = padded[:, 1:, :-1] - padded[:, :-1, :-1]
    flux_east = coeffs[0, :-1, :-1] * east_diff + coeffs[1, :-1, :-1] * north_diff
    flux_north = coeffs[1, :-1, :-1] * east_diff + coeffs[2, :-1, :-1] * north_diff
    return flux_east[:, 1:, 1:] - flux_east[:, 1:, :-1] + (flux_north[:, 1:, 1:] - flux_north[:, :-1, 1:])

def forward_section(padded, coeffs):
    return padded[:, 1:-1, 1:-1] + time_step * coeffs[3, 1:-1, 1:-1] * divergence(padded, coeffs)

def pad_grid(values):
    wrapped = jnp.concatenate([values[:, :, -1:], values, values[:, :, :1]], axis=2)
    return jnp.pad(wrapped, ((0, 0), (1, 1), (0, 0)))

def spread(values, coefficients):
    return forward_section(pad_grid(values), pad_grid(coefficients))

def reference(panels, eof_basis, control, coefficients):
    fields, eof_count, row_count, col_count = control.shape
    flattened = control.reshape(fields * eof_count, row_count, col_count)
    zero_state = jnp.zeros_like(flattened)
    _, backward = jax.vjp(lambda values: spread(values, coefficients), zero_state)
    adjointed = flattened
    for repeat in range(STEPS):
        adjointed = backward(adjointed)[0]
    weights = adjointed.reshape(fields, eof_count, row_count, col_count)
    basis = eof_basis.astype(jnp.float32)

    def member_term(combined, member_panel):
        projected = jnp.einsum('flyx,fle->feyx', member_panel.astype(jnp.float32), basis, precision=lax.Precision.HIGHEST)
        scores = lax.optimization_barrier(jnp.sum(projected * weights, axis=(0, 1)))
        return (combined + projected * scores, None)
    combined, _ = lax.scan(member_term, jnp.zeros(weights.shape, jnp.float32), panels)
    combined = combined / (M - 1)
    values = combined.reshape(fields * eof_count, row_count, col_count)
    for repeat in range(STEPS):
        values = spread(values, coefficients)
    return values.reshape(fields, eof_count, row_count, col_count)
```

```python
import functools

import jax
import jax.numpy as jnp
from jax import lax
from jax.experimental import pallas as pl
from jax.experimental.pallas import tpu as pltpu
from jax.sharding import PartitionSpec as P

STEPS = 6
TIME_STEP = 0.09
ROWS = 8
COLS = 128
DEPTH = STEPS
EXT = ROWS + 2 * DEPTH
SLOT = COLS // ROWS
PLANES = 40
WIDE = 48
MESH = pl.DeviceIdType.MESH


def adjoint_steps(grid, coef):
    def one_step(_, carry):
        def weighted(r):
            return coef[r, 3][None] * grid[r]

        below = None
        here = weighted(0)
        for r in range(EXT - 1):
            above = weighted(r + 1)
            east = pltpu.roll(here, 2 * COLS - 1, 2) - here
            north = above - here
            kxy = coef[r, 1][None]
            flux_north = kxy * east + coef[r, 2][None] * north
            if r > 0:
                flux_east = coef[r, 0][None] * east + kxy * north
                grid[r] = grid[r] + (
                    (flux_east - pltpu.roll(flux_east, 1, 2)) + (flux_north - below)
                )
            below = flux_north
            here = above
        return carry

    lax.fori_loop(0, STEPS, one_step, 0)


def forward_steps(grid, coef):
    def one_step(_, carry):
        below = None
        here = grid[0]
        for r in range(EXT - 1):
            above = grid[r + 1]
            east = pltpu.roll(here, 2 * COLS - 1, 2) - here
            north = above - here
            kxy = coef[r, 1][None]
            flux_north = kxy * east + coef[r, 2][None] * north
            if r > 0:
                flux_east = coef[r, 0][None] * east + kxy * north
                grid[r] = here + coef[r, 3][None] * (
                    (flux_east - pltpu.roll(flux_east, 1, 2)) + (flux_north - below)
                )
            below = flux_north
            here = above
        return carry

    lax.fori_loop(0, STEPS, one_step, 0)


def kernel(
    sizes,
    panels_hbm,
    eof_hbm,
    control_hbm,
    coef_hbm,
    out_ref,
    control,
    coef_in,
    eof,
    panel,
    weight,
    projected,
    grid,
    coef,
    tile_a,
    edge_a,
    north_a,
    south_a,
    side_a,
    tile_b,
    edge_b,
    north_b,
    south_b,
    side_b,
    local_sem,
    send_sem,
    recv_sem,
):
    count_x, count_y, count_z = sizes
    gx, gy, gz = lax.axis_index("gx"), lax.axis_index("gy"), lax.axis_index("gz")
    place = gx * count_z + gz
    total = count_x * count_z
    east = lax.rem(place + 1, total)
    west = lax.rem(place + total - 1, total)
    up = lax.rem(gy + 1, count_y)
    down = lax.rem(gy + count_y - 1, count_y)

    def at(column, row):
        return (column // count_z, row, lax.rem(column, count_z))

    sides = [at(east, gy), at(west, gy), at(east, up), at(west, up), at(east, down), at(west, down)]
    peers = [(gx, gy, lax.rem(gz + d, count_z)) for d in range(1, count_z)]
    north_id, south_id = at(place, up), at(place, down)

    copies = [
        pltpu.make_async_copy(control_hbm, control, local_sem.at[0]),
        pltpu.make_async_copy(coef_hbm, coef_in.at[pl.ds(0, 32)], local_sem.at[1]),
        pltpu.make_async_copy(coef_hbm, coef_in.at[pl.ds(32, 32)], local_sem.at[2]),
        pltpu.make_async_copy(eof_hbm, eof, local_sem.at[3]),
    ]
    for copy in copies:
        copy.start()

    levels = panel.shape[1] // count_z
    mine = pl.ds(pl.multiple_of(gz * levels, levels), levels)
    own_panel = pltpu.make_async_copy(
        panels_hbm.at[:, :, pl.ds(pl.multiple_of(gz * COLS, COLS), COLS)],
        panel.at[:, mine, :],
        local_sem.at[4],
    )
    own_panel.start()

    barrier = pltpu.get_barrier_semaphore()
    partners = sides + [north_id, south_id] + peers
    for partner in partners:
        pl.semaphore_signal(barrier, inc=1, device_id=partner, device_id_type=MESH)

    lane = lax.broadcasted_iota(jnp.int32, (WIDE, COLS), 1)
    sub8 = lax.broadcasted_iota(jnp.int32, (8, COLS), 0)
    for copy in copies[:3]:
        copy.wait()

    edge = jnp.zeros((WIDE, COLS), jnp.float32)
    for y in range(ROWS):
        fields = control[pl.ds(y, PLANES, stride=ROWS), :]
        grid[DEPTH + y, :, :, 0:COLS] = fields.reshape(5, 8, COLS)
        entries = coef_in[pl.ds(y, 8, stride=ROWS), :]
        for k in range(4):
            scale = TIME_STEP if k == 3 else 1.0
            coef[DEPTH + y, k, :, 0:COLS] = jnp.broadcast_to(scale * entries[k : k + 1], (8, COLS))
        high = entries.astype(jnp.bfloat16).astype(jnp.float32)
        row = jnp.concatenate([fields, jnp.where(sub8 < 4, high, entries - high)], axis=0)
        tile_a[y] = row.astype(jnp.bfloat16)
        shifted = pltpu.roll(row, SLOT * y + SLOT // 2, 1)
        edge = jnp.where((lane >= SLOT * y) & (lane < SLOT * (y + 1)), shifted, edge)
    edge_a[...] = edge.astype(jnp.bfloat16)

    def exchange(first, tile, edge, north, south, side):
        moves = [(edge, side.at[k], sides[k]) for k in range(6)]
        moves = [
            (tile.at[pl.ds(ROWS - DEPTH, DEPTH)], south, north_id),
            (tile.at[pl.ds(0, DEPTH)], north, south_id),
        ] + moves
        return [
            pltpu.make_async_remote_copy(
                src_ref=source,
                dst_ref=target,
                send_sem=send_sem.at[first + k],
                recv_sem=recv_sem.at[first + k],
                device_id=device,
                device_id_type=MESH,
            )
            for k, (source, target, device) in enumerate(moves)
        ]

    pl.semaphore_wait(barrier, len(partners))
    halo_a = exchange(0, tile_a, edge_a, north_a, south_a, side_a)
    for copy in halo_a:
        copy.start()
    sent_panels = []
    for d in range(1, count_z):
        peer = lax.rem(gz + d, count_z)
        copy = pltpu.make_async_remote_copy(
            src_ref=panels_hbm.at[:, :, pl.ds(pl.multiple_of(peer * COLS, COLS), COLS)],
            dst_ref=panel.at[:, mine, :],
            send_sem=send_sem.at[16 + d],
            recv_sem=recv_sem.at[16 + d],
            device_id=peers[d - 1],
            device_id_type=MESH,
        )
        copy.start()
        sent_panels.append(copy)

    copies[3].wait()
    plane_of = lax.broadcasted_iota(jnp.int32, (PLANES, 10), 0)
    eof_of = lax.broadcasted_iota(jnp.int32, (PLANES, 10), 1)

    def field_of(plane):
        one = jnp.ones_like(plane)
        none = jnp.zeros_like(plane)
        found = jnp.where(plane >= 10, one, none)
        found = found + jnp.where(plane >= 20, one, none)
        return found + jnp.where(plane >= 30, one, none)

    pick = jnp.where(plane_of - 10 * field_of(plane_of) == eof_of, 1.0, 0.0).astype(jnp.bfloat16)
    by_plane = lax.dot_general(
        pick, eof[...], (((1,), (1,)), ((), ())), preferred_element_type=jnp.float32
    )
    plane_row = lax.broadcasted_iota(jnp.int32, (PLANES, 64), 0)
    level_col = lax.broadcasted_iota(jnp.int32, (PLANES, 64), 1)
    by_plane = jnp.where(field_of(plane_row) == lax.shift_right_logical(level_col, 4), by_plane, 0.0)
    level_row = lax.broadcasted_iota(jnp.int32, (64, 512), 0)
    spot = lax.broadcasted_iota(jnp.int32, (64, 512), 1)
    source = lax.shift_right_logical(spot, 7)
    field = lax.shift_right_logical(spot, 5) & 3
    level = lax.shift_right_logical(spot, 3) & 3
    repeat = jnp.where(level_row == field * 16 + source * 4 + level, 1.0, 0.0).astype(jnp.bfloat16)
    spread = jnp.dot(by_plane.astype(jnp.bfloat16), repeat, preferred_element_type=jnp.float32)
    spread_row = lax.broadcasted_iota(jnp.int32, (PLANES, 512), 1) & 7
    for pair in range(ROWS // 2):
        both = [jnp.where(spread_row == 2 * pair + k, spread, 0.0) for k in range(2)]
        weight[pl.ds(2 * PLANES * pair, 2 * PLANES), :] = jnp.concatenate(both, axis=0).astype(jnp.bfloat16)

    keep_north = jnp.where(gy < count_y - 1, 1.0, 0.0).astype(jnp.float32)
    keep_south = jnp.where(gy > 0, 1.0, 0.0).astype(jnp.float32)

    def halo_rows(north, south, side, planes):
        from_west = (lax.broadcasted_iota(jnp.int32, (planes, COLS), 1) & (SLOT - 1)) < SLOT // 2

        def edges(a, b):
            return jnp.where(
                from_west, side[a].astype(jnp.float32), side[b].astype(jnp.float32)
            )

        def slot(pack, y):
            return pltpu.roll(pack, COLS - SLOT // 2 - SLOT * y, 1)

        pack = edges(0, 1)
        for y in range(ROWS):
            yield DEPTH + y, None, slot(pack, y)
        pack = edges(2, 3) * keep_south
        for y in range(DEPTH):
            block = south[y].astype(jnp.float32) * keep_south
            yield y, block, slot(pack, y + ROWS - DEPTH)
        pack = edges(4, 5) * keep_north
        for y in range(DEPTH):
            block = north[y].astype(jnp.float32) * keep_north
            yield DEPTH + ROWS + y, block, slot(pack, y)

    def put(row, start, block):
        columns = slice(start, start + COLS)
        grid[row, :, :, columns] = block[0:PLANES].reshape(5, 8, COLS)

    def put_coef(row, start, block):
        parts = block[PLANES:WIDE]
        entries = parts + pltpu.roll(parts, 4, 0)
        for k in range(4):
            scale = TIME_STEP if k == 3 else 1.0
            coef[row, k, :, start : start + COLS] = jnp.broadcast_to(
                scale * entries[k : k + 1], (8, COLS)
            )

    for copy in halo_a:
        copy.wait_recv()
    for row, block, side in halo_rows(north_a, south_a, side_a, WIDE):
        if block is not None:
            put(row, 0, block)
            put_coef(row, 0, block)
        put(row, COLS, side)
        put_coef(row, COLS, side)
    adjoint_steps(grid, coef)

    own_panel.wait()
    for copy in sent_panels:
        copy.wait_recv()
    members = panel.shape[0]
    for m in range(0, members, 2):
        pair = jnp.concatenate([panel[m], panel[m + 1]], axis=1)
        projected[:, m * COLS : (m + 2) * COLS] = jnp.dot(
            weight[...], pair, preferred_element_type=jnp.float32
        )

    edge = jnp.zeros((PLANES, COLS), jnp.float32)
    lane = lax.broadcasted_iota(jnp.int32, (PLANES, COLS), 1)
    for y in range(ROWS):
        factor = grid[DEPTH + y, :, :, 0:COLS].reshape(PLANES, COLS)
        row = None
        for m in range(members):
            term = projected[y * PLANES : (y + 1) * PLANES, m * COLS : (m + 1) * COLS]
            score = jnp.sum(term * factor, axis=0, keepdims=True) * (1.0 / (members - 1))
            row = term * score if row is None else row + term * score
        grid[DEPTH + y, :, :, 0:COLS] = row.reshape(5, 8, COLS)
        tile_b[y] = row.astype(jnp.bfloat16)
        shifted = pltpu.roll(row, SLOT * y + SLOT // 2, 1)
        edge = jnp.where((lane >= SLOT * y) & (lane < SLOT * (y + 1)), shifted, edge)
    edge_b[...] = edge.astype(jnp.bfloat16)

    halo_b = exchange(8, tile_b, edge_b, north_b, south_b, side_b)
    for copy in halo_b:
        copy.start()
    for copy in halo_b:
        copy.wait_recv()
    for row, block, side in halo_rows(north_b, south_b, side_b, PLANES):
        if block is not None:
            put(row, 0, block)
        put(row, COLS, side)
    forward_steps(grid, coef)

    for y in range(ROWS):
        out_ref[pl.ds(y, PLANES, stride=ROWS), :] = grid[DEPTH + y, :, :, 0:COLS].reshape(PLANES, COLS)
    for copy in halo_a + sent_panels + halo_b:
        copy.wait_send()


def solution(mesh):
    sizes = tuple(mesh.shape[name] for name in ("gx", "gy", "gz"))

    def per_device(panels, eof_basis, control, coefficients):
        members, fields, levels, rows, columns = panels.shape
        eof_count = eof_basis.shape[2]
        deep = fields * levels * rows
        f32, bf16 = jnp.float32, jnp.bfloat16
        anywhere = pl.BlockSpec(memory_space=pl.ANY)
        out = pl.pallas_call(
            functools.partial(kernel, sizes),
            out_shape=jax.ShapeDtypeStruct((PLANES * ROWS, COLS), f32),
            in_specs=[anywhere] * 4,
            out_specs=pl.BlockSpec(memory_space=pltpu.VMEM),
            scratch_shapes=[
                pltpu.VMEM((PLANES * ROWS, COLS), f32),
                pltpu.VMEM((8 * ROWS, COLS), f32),
                pltpu.VMEM((fields * levels * sizes[2], eof_count), bf16),
                pltpu.VMEM((members, deep * sizes[2], COLS), bf16),
                pltpu.VMEM((PLANES * ROWS, deep * sizes[2]), bf16),
                pltpu.VMEM((PLANES * ROWS, members * COLS), f32),
                pltpu.VMEM((EXT, 5, 8, 2 * COLS), f32),
                pltpu.VMEM((EXT, 4, 8, 2 * COLS), f32),
                pltpu.VMEM((ROWS, WIDE, COLS), bf16),
                pltpu.VMEM((WIDE, COLS), bf16),
                pltpu.VMEM((DEPTH, WIDE, COLS), bf16),
                pltpu.VMEM((DEPTH, WIDE, COLS), bf16),
                pltpu.VMEM((6, WIDE, COLS), bf16),
                pltpu.VMEM((ROWS, PLANES, COLS), bf16),
                pltpu.VMEM((PLANES, COLS), bf16),
                pltpu.VMEM((DEPTH, PLANES, COLS), bf16),
                pltpu.VMEM((DEPTH, PLANES, COLS), bf16),
                pltpu.VMEM((6, PLANES, COLS), bf16),
                pltpu.SemaphoreType.DMA((5,)),
                pltpu.SemaphoreType.DMA((20,)),
                pltpu.SemaphoreType.DMA((20,)),
            ],
            compiler_params=pltpu.CompilerParams(
                collective_id=0, has_side_effects=True, vmem_limit_bytes=32 * 1024 * 1024
            ),
            name="covariance",
        )(
            panels.reshape(members, deep, columns),
            eof_basis.reshape(-1, eof_count),
            control.reshape(-1, COLS),
            coefficients.reshape(-1, COLS),
        )
        return out.reshape(control.shape)

    in_specs = (
        P(None, None, "gz", "gy", "gx"),
        P(),
        P(None, None, "gy", ("gx", "gz")),
        P(None, "gy", ("gx", "gz")),
    )
    return jax.shard_map(
        per_device,
        mesh=mesh,
        in_specs=in_specs,
        out_specs=P(None, None, "gy", ("gx", "gz")),
        check_vma=False,
    )
```

```python
import functools

import jax
import jax.numpy as jnp
from jax import lax
from jax.experimental import pallas as pl
from jax.experimental.pallas import tpu as pltpu
from jax.sharding import PartitionSpec as P

STEPS = 6
TIME_STEP = 0.09
ROWS = 8
COLS = 128
DEPTH = STEPS
EXT = ROWS + 2 * DEPTH
SLOT = COLS // ROWS
HALF = SLOT // 2
PLANES = 40
GROUPS = PLANES // 8
LAG = 2
CHUNKS_A = ((0, 2), (2, 4), (4, 6))
CHUNKS_B = ((0, 2), (2, 4), (4, 5))
MESH = pl.DeviceIdType.MESH


def diffuse(grid, coef, group, forward):
    level = [{} for _ in range(STEPS + 1)]
    below = [None] * STEPS
    weighted = [{} for _ in range(STEPS)]

    def source(k, r):
        if r not in weighted[k]:
            weighted[k][r] = level[k][r] if forward else coef[r, 3] * level[k][r]
        return weighted[k][r]

    def update(k, r):
        here, above = source(k, r), source(k, r + 1)
        east = pltpu.roll(here, 2 * COLS - 1, 1) - here
        north = above - here
        kxy = coef[r, 1]
        flux_north = kxy * east + coef[r, 2] * north
        if r > k:
            flux_east = coef[r, 0] * east + kxy * north
            div = (flux_east - pltpu.roll(flux_east, 1, 1)) + (flux_north - below[k])
            old = level[k][r]
            new = old + coef[r, 3] * div if forward else old + div
            if k == STEPS - 1:
                grid[group, r] = new
            else:
                level[k + 1][r] = new
        below[k] = flux_north

    level[0][0] = grid[group, 0]
    for top in range(1, EXT + LAG * STEPS):
        if top < EXT:
            level[0][top] = grid[group, top]
        for k in range(STEPS):
            r = top - 1 - LAG * k
            if k <= r <= EXT - 2 - k:
                update(k, r)


def kernel(
    sizes,
    panels_hbm,
    eof_hbm,
    control_hbm,
    coef_hbm,
    out_ref,
    control,
    coef_in,
    eof,
    basis,
    panel,
    weight,
    projected,
    grid,
    coef,
    tile_a,
    edge_a,
    north_a,
    south_a,
    side_a,
    tile_b,
    edge_b,
    north_b,
    south_b,
    side_b,
    local_sem,
    send_sem,
    recv_sem,
):
    count_x, count_y, count_z = sizes
    gx, gy, gz = lax.axis_index("gx"), lax.axis_index("gy"), lax.axis_index("gz")
    place = gx * count_z + gz
    total = count_x * count_z
    east = lax.rem(place + 1, total)
    west = lax.rem(place + total - 1, total)
    up = lax.rem(gy + 1, count_y)
    down = lax.rem(gy + count_y - 1, count_y)

    def at(column, row):
        return (column // count_z, row, lax.rem(column, count_z))

    sides = [at(east, gy), at(west, gy), at(east, up), at(west, up), at(east, down), at(west, down)]
    peers = [(gx, gy, lax.rem(gz + d, count_z)) for d in range(1, count_z)]
    north_id, south_id = at(place, up), at(place, down)

    barrier = pltpu.get_barrier_semaphore()
    partners = sides + [north_id, south_id] + peers
    for partner in partners:
        pl.semaphore_signal(barrier, inc=1, device_id=partner, device_id_type=MESH)

    copies = [
        pltpu.make_async_copy(control_hbm, control, local_sem.at[0]),
        pltpu.make_async_copy(coef_hbm, coef_in.at[pl.ds(0, 32)], local_sem.at[1]),
        pltpu.make_async_copy(coef_hbm, coef_in.at[pl.ds(32, 32)], local_sem.at[2]),
        pltpu.make_async_copy(eof_hbm, eof, local_sem.at[3]),
    ]
    for copy in copies:
        copy.start()
    levels = panel.shape[1] // count_z
    mine = pl.ds(pl.multiple_of(gz * levels, levels), levels)
    own_panel = pltpu.make_async_copy(
        panels_hbm.at[:, :, pl.ds(pl.multiple_of(gz * COLS, COLS), COLS)],
        panel.at[:, mine, :],
        local_sem.at[4],
    )
    own_panel.start()

    lane = lax.broadcasted_iota(jnp.int32, (8, COLS), 1)
    first_half = (lane & (SLOT - 1)) < HALF
    sub8 = lax.broadcasted_iota(jnp.int32, (8, COLS), 0)
    slots = [(lane >= SLOT * y) & (lane < SLOT * (y + 1)) for y in range(ROWS)]

    def slotted(edges, y, blocks):
        for g, block in enumerate(blocks):
            shifted = pltpu.roll(block, SLOT * y + HALF, 1)
            edges[g] = shifted if edges[g] is None else jnp.where(slots[y], shifted, edges[g])

    def pack_edges(edges, edge):
        for pair in range(0, len(edges), 2):
            one = edges[pair]
            two = edges[pair + 1] if pair + 1 < len(edges) else one
            easting = jnp.where(first_half, one, pltpu.roll(two, HALF, 1))
            westing = jnp.where(first_half, pltpu.roll(one, COLS - HALF, 1), two)
            edge[0, pair // 2] = easting.astype(jnp.bfloat16)
            edge[1, pair // 2] = westing.astype(jnp.bfloat16)

    for copy in copies[:3]:
        copy.wait()
    edges = [None] * (GROUPS + 1)
    for y in range(ROWS):
        fields = control[pl.ds(y, PLANES, stride=ROWS), :]
        entries = coef_in[pl.ds(y, 8, stride=ROWS), :]
        high = entries.astype(jnp.bfloat16).astype(jnp.float32)
        blocks = [jnp.where(sub8 < 4, high, entries - high)]
        blocks += [fields[8 * g : 8 * g + 8] for g in range(GROUPS)]
        for g, block in enumerate(blocks):
            tile_a[g, y] = block.astype(jnp.bfloat16)
        slotted(edges, y, blocks)
    pack_edges(edges, edge_a)

    def exchange(first, chunks, tile, edge, north, south, side):
        moves = [(edge.at[k % 2], side.at[k], sides[k]) for k in range(6)]
        for a, b in chunks:
            groups = pl.ds(a, b - a)
            moves.append((tile.at[groups, pl.ds(ROWS - DEPTH, DEPTH)], south.at[groups], north_id))
            moves.append((tile.at[groups, pl.ds(0, DEPTH)], north.at[groups], south_id))
        return [
            pltpu.make_async_remote_copy(
                src_ref=source,
                dst_ref=target,
                send_sem=send_sem.at[first + k],
                recv_sem=recv_sem.at[first + k],
                device_id=device,
                device_id_type=MESH,
            )
            for k, (source, target, device) in enumerate(moves)
        ]

    pl.semaphore_wait(barrier, len(partners))
    halo_a = exchange(0, CHUNKS_A, tile_a, edge_a, north_a, south_a, side_a)
    for copy in halo_a:
        copy.start()
    sent_panels = []
    for d in range(1, count_z):
        peer = lax.rem(gz + d, count_z)
        copy = pltpu.make_async_remote_copy(
            src_ref=panels_hbm.at[:, :, pl.ds(pl.multiple_of(peer * COLS, COLS), COLS)],
            dst_ref=panel.at[:, mine, :],
            send_sem=send_sem.at[31 + d],
            recv_sem=recv_sem.at[31 + d],
            device_id=peers[d - 1],
            device_id_type=MESH,
        )
        copy.start()
        sent_panels.append(copy)

    def put_coef(row, start, entries):
        for k in range(4):
            scale = TIME_STEP if k == 3 else 1.0
            coef[row, k, :, start : start + COLS] = jnp.broadcast_to(
                scale * entries[k : k + 1], (8, COLS)
            )

    for y in range(ROWS):
        fields = control[pl.ds(y, PLANES, stride=ROWS), :]
        for g in range(GROUPS):
            grid[g, DEPTH + y, :, 0:COLS] = fields[8 * g : 8 * g + 8]
        put_coef(DEPTH + y, 0, coef_in[pl.ds(y, 8, stride=ROWS), :])

    copies[3].wait()
    count_e, count_f, count_l = eof.shape
    for e in range(count_e):
        block = eof[e].astype(jnp.float32)
        for f in range(count_f):
            basis[f * count_e + e : f * count_e + e + 1, :] = block[f : f + 1]
    plane = lax.broadcasted_iota(jnp.int32, (PLANES, 512), 0)
    field_of = jnp.zeros_like(plane)
    for f in range(1, count_f):
        field_of = field_of + jnp.where(plane >= f * count_e, 1, 0)
    spot = lax.broadcasted_iota(jnp.int32, (PLANES, 512), 1)
    same_field = field_of == (lax.shift_right_logical(spot, 5) & 3)
    level_row = lax.broadcasted_iota(jnp.int32, (count_l, 512), 0)
    level_spot = lax.broadcasted_iota(jnp.int32, (count_l, 512), 1)
    level_of = 4 * lax.shift_right_logical(level_spot, 7) + (lax.shift_right_logical(level_spot, 3) & 3)
    repeat = jnp.where(level_row == level_of, 1.0, 0.0).astype(jnp.bfloat16)
    spread = jnp.dot(basis[...].astype(jnp.bfloat16), repeat, preferred_element_type=jnp.float32)
    spread = jnp.where(same_field, spread, 0.0)
    for pair in range(ROWS // 2):
        both = [jnp.where((spot & 7) == 2 * pair + k, spread, 0.0) for k in range(2)]
        weight[pl.ds(2 * PLANES * pair, 2 * PLANES), :] = jnp.concatenate(both, axis=0).astype(jnp.bfloat16)

    keep_north = jnp.where(gy < count_y - 1, 1.0, 0.0).astype(jnp.float32)
    keep_south = jnp.where(gy > 0, 1.0, 0.0).astype(jnp.float32)
    ranges = (
        (DEPTH, 0, 0, ROWS, None),
        (0, 2, ROWS - DEPTH, DEPTH, keep_south),
        (DEPTH + ROWS, 4, 0, DEPTH, keep_north),
    )

    def edge_rows(side, group):
        for start, k, slot, count, keep in ranges:
            from_west = side[k, group // 2].astype(jnp.float32)
            from_east = side[k + 1, group // 2].astype(jnp.float32)
            if group % 2 == 0:
                pack = jnp.where(first_half, from_west, pltpu.roll(from_east, HALF, 1))
            else:
                pack = jnp.where(first_half, pltpu.roll(from_west, COLS - HALF, 1), from_east)
            if keep is not None:
                pack = pack * keep
            for y in range(count):
                yield start + y, pltpu.roll(pack, COLS - HALF - SLOT * (y + slot), 1)

    def halo_rows(north, south, group):
        for y in range(DEPTH):
            yield y, south[group, y].astype(jnp.float32) * keep_south
            yield DEPTH + ROWS + y, north[group, y].astype(jnp.float32) * keep_north

    def joined(parts):
        return parts + pltpu.roll(parts, 4, 0)

    for copy in halo_a[:6]:
        copy.wait_recv()
    for row, block in edge_rows(side_a, 0):
        put_coef(row, COLS, joined(block))
    for g in range(GROUPS):
        for row, block in edge_rows(side_a, g + 1):
            grid[g, row, :, COLS:] = block
    for i, (a, b) in enumerate(CHUNKS_A):
        for copy in halo_a[6 + 2 * i : 8 + 2 * i]:
            copy.wait_recv()
        for g in range(a, b):
            for row, block in halo_rows(north_a, south_a, g):
                if g == 0:
                    put_coef(row, 0, joined(block))
                else:
                    grid[g - 1, row, :, 0:COLS] = block

        def step_a(g, carry):
            diffuse(grid, coef, g, False)
            return carry

        lax.fori_loop(max(a - 1, 0), b - 1, step_a, 0)

    own_panel.wait()
    for copy in sent_panels:
        copy.wait_recv()
    members = panel.shape[0]
    for m in range(0, members, 2):
        pair = jnp.concatenate([panel[m], panel[m + 1]], axis=1)
        projected[:, m * COLS : (m + 2) * COLS] = jnp.dot(
            weight[...], pair, preferred_element_type=jnp.float32
        )

    edges = [None] * GROUPS
    for y in range(ROWS):
        factor = jnp.concatenate([grid[g, DEPTH + y, :, 0:COLS] for g in range(GROUPS)], axis=0)
        row = None
        for m in range(members):
            term = projected[y * PLANES : (y + 1) * PLANES, m * COLS : (m + 1) * COLS]
            score = jnp.sum(term * factor, axis=0, keepdims=True) * (1.0 / (members - 1))
            row = term * score if row is None else row + term * score
        blocks = [row[8 * g : 8 * g + 8] for g in range(GROUPS)]
        for g, block in enumerate(blocks):
            grid[g, DEPTH + y, :, 0:COLS] = block
            tile_b[g, y] = block.astype(jnp.bfloat16)
        slotted(edges, y, blocks)
    pack_edges(edges, edge_b)

    first_b = 6 + 2 * len(CHUNKS_A)
    halo_b = exchange(first_b, CHUNKS_B, tile_b, edge_b, north_b, south_b, side_b)
    for copy in halo_b:
        copy.start()
    for copy in halo_b[:6]:
        copy.wait_recv()
    for g in range(GROUPS):
        for row, block in edge_rows(side_b, g):
            grid[g, row, :, COLS:] = block
    for i, (a, b) in enumerate(CHUNKS_B):
        for copy in halo_b[6 + 2 * i : 8 + 2 * i]:
            copy.wait_recv()
        for g in range(a, b):
            for row, block in halo_rows(north_b, south_b, g):
                grid[g, row, :, 0:COLS] = block

        def step_b(g, carry):
            diffuse(grid, coef, g, True)
            return carry

        lax.fori_loop(a, b, step_b, 0)
        for g in range(a, b):
            for y in range(ROWS):
                out_ref[pl.ds(8 * ROWS * g + y, 8, stride=ROWS), :] = grid[g, DEPTH + y, :, 0:COLS]
    for copy in halo_a + sent_panels + halo_b:
        copy.wait_send()


def solution(mesh):
    sizes = tuple(mesh.shape[name] for name in ("gx", "gy", "gz"))

    def per_device(panels, eof_basis, control, coefficients):
        members, fields, levels, rows, columns = panels.shape
        eof_count = eof_basis.shape[2]
        deep = fields * levels * rows
        f32, bf16 = jnp.float32, jnp.bfloat16
        anywhere = pl.BlockSpec(memory_space=pl.ANY)
        wide = GROUPS + 1
        pairs_a, pairs_b = wide // 2, (GROUPS + 1) // 2
        out = pl.pallas_call(
            functools.partial(kernel, sizes),
            out_shape=jax.ShapeDtypeStruct((PLANES * ROWS, COLS), f32),
            in_specs=[anywhere] * 4,
            out_specs=pl.BlockSpec(memory_space=pltpu.VMEM),
            scratch_shapes=[
                pltpu.VMEM((PLANES * ROWS, COLS), f32),
                pltpu.VMEM((8 * ROWS, COLS), f32),
                pltpu.VMEM((eof_count, fields, levels * sizes[2]), bf16),
                pltpu.VMEM((PLANES, levels * sizes[2]), f32),
                pltpu.VMEM((members, deep * sizes[2], COLS), bf16),
                pltpu.VMEM((PLANES * ROWS, deep * sizes[2]), bf16),
                pltpu.VMEM((PLANES * ROWS, members * COLS), f32),
                pltpu.VMEM((GROUPS, EXT, 8, 2 * COLS), f32),
                pltpu.VMEM((EXT, 4, 8, 2 * COLS), f32),
                pltpu.VMEM((wide, ROWS, 8, COLS), bf16),
                pltpu.VMEM((2, pairs_a, 8, COLS), bf16),
                pltpu.VMEM((wide, DEPTH, 8, COLS), bf16),
                pltpu.VMEM((wide, DEPTH, 8, COLS), bf16),
                pltpu.VMEM((6, pairs_a, 8, COLS), bf16),
                pltpu.VMEM((GROUPS, ROWS, 8, COLS), bf16),
                pltpu.VMEM((2, pairs_b, 8, COLS), bf16),
                pltpu.VMEM((GROUPS, DEPTH, 8, COLS), bf16),
                pltpu.VMEM((GROUPS, DEPTH, 8, COLS), bf16),
                pltpu.VMEM((6, pairs_b, 8, COLS), bf16),
                pltpu.SemaphoreType.DMA((5,)),
                pltpu.SemaphoreType.DMA((36,)),
                pltpu.SemaphoreType.DMA((36,)),
            ],
            compiler_params=pltpu.CompilerParams(
                collective_id=0, has_side_effects=True, vmem_limit_bytes=63 * 1024 * 1024
            ),
            name="covariance",
        )(
            panels.reshape(members, deep, columns),
            eof_basis.transpose(2, 0, 1),
            control.reshape(-1, COLS),
            coefficients.reshape(-1, COLS),
        )
        return out.reshape(control.shape)

    in_specs = (
        P(None, None, "gz", "gy", "gx"),
        P(),
        P(None, None, "gy", ("gx", "gz")),
        P(None, "gy", ("gx", "gz")),
    )
    return jax.shard_map(
        per_device,
        mesh=mesh,
        in_specs=in_specs,
        out_specs=P(None, None, "gy", ("gx", "gz")),
        check_vma=False,
    )
```

```python
import functools

import jax
import jax.numpy as jnp
from jax import lax
from jax.experimental import pallas as pl
from jax.experimental.pallas import tpu as pltpu
from jax.sharding import PartitionSpec as P

STEPS = 6
TIME_STEP = 0.09
ROWS = 8
COLS = 128
DEPTH = STEPS
EXT = ROWS + 2 * DEPTH
SLOT = COLS // ROWS
HALF = SLOT // 2
PLANES = 40
GROUPS = PLANES // 8
LAG = 2
LINES = 7
TALL = COLS + 16
STRIDE = 24
CHUNKS_A = ((0, 1), (1, 3), (3, 5))
CHUNKS_B = ((0, GROUPS),)
MESH = pl.DeviceIdType.MESH


def adjoint_steps(grid, coef, group):
    level = [{} for _ in range(STEPS + 1)]
    below = [None] * STEPS
    weighted = [{} for _ in range(STEPS)]

    def source(k, r):
        if r not in weighted[k]:
            weighted[k][r] = coef[r, 3] * level[k][r]
        return weighted[k][r]

    def update(k, r):
        here, above = source(k, r), source(k, r + 1)
        east = pltpu.roll(here, 2 * COLS - 1, 1) - here
        north = above - here
        kxy = coef[r, 1]
        flux_north = kxy * east + coef[r, 2] * north
        if r > k:
            flux_east = coef[r, 0] * east + kxy * north
            div = (flux_east - pltpu.roll(flux_east, 1, 1)) + (flux_north - below[k])
            old = level[k][r]
            new = old + div
            if k == STEPS - 1:
                grid[group, r] = new
            else:
                level[k + 1][r] = new
        below[k] = flux_north

    level[0][0] = grid[group, 0]
    for top in range(1, EXT + LAG * STEPS):
        if top < EXT:
            level[0][top] = grid[group, top]
        for k in range(STEPS):
            r = top - 1 - LAG * k
            if k <= r <= EXT - 2 - k:
                update(k, r)


def forward_steps(turned, flux, coef_t):
    part = TALL // 3

    def one_step(_, carry):
        for c in range(3):
            rows = pl.ds(part * c, part)
            ahead = pl.ds(part * c + 1, part)
            behind = pl.ds(8 + part * c - 1, part)
            stored = pl.ds(8 + part * c, part)

            def flux_of(g, here, above):
                east = turned[g, ahead] - here
                north = above - here
                kxy = coef_t[1, g, rows]
                return coef_t[0, g, rows] * east + kxy * north, kxy * east + coef_t[2, g, rows] * north

            last = turned[LINES - 1, rows]
            after_last = pltpu.roll(turned[0, rows], COLS - PLANES, 1)
            last_east, last_north = flux_of(LINES - 1, last, after_last)
            below = pltpu.roll(last_north, PLANES, 1)
            here = turned[0, rows]
            for g in range(LINES):
                if g < LINES - 1:
                    above = turned[g + 1, rows]
                    flux_east, flux_north = flux_of(g, here, above)
                else:
                    flux_east, flux_north = last_east, last_north
                flux[g, stored] = flux_east
                turned[g, rows] = here + coef_t[3, g, rows] * (
                    (flux_east - flux[g, behind]) + (flux_north - below)
                )
                below = flux_north
                here = above
        return carry

    lax.fori_loop(0, STEPS, one_step, 0)


def kernel(
    sizes,
    panels_hbm,
    eof_hbm,
    control_hbm,
    coef_hbm,
    out_ref,
    control,
    coef_in,
    eof,
    basis,
    panel,
    weight,
    projected,
    grid,
    coef,
    tile_c,
    north_c,
    south_c,
    tile_a,
    edge_a,
    north_a,
    south_a,
    side_a,
    tile_b,
    edge_b,
    north_b,
    south_b,
    side_b,
    own_b,
    turned,
    flux,
    coef_rows,
    coef_t,
    local_sem,
    send_sem,
    recv_sem,
):
    count_x, count_y, count_z = sizes
    gx, gy, gz = lax.axis_index("gx"), lax.axis_index("gy"), lax.axis_index("gz")
    place = gx * count_z + gz
    total = count_x * count_z
    east = lax.rem(place + 1, total)
    west = lax.rem(place + total - 1, total)
    up = lax.rem(gy + 1, count_y)
    down = lax.rem(gy + count_y - 1, count_y)

    def at(column, row):
        return (column // count_z, row, lax.rem(column, count_z))

    sides = [at(east, gy), at(west, gy), at(east, up), at(west, up), at(east, down), at(west, down)]
    peers = [(gx, gy, lax.rem(gz + d, count_z)) for d in range(1, count_z)]
    north_id, south_id = at(place, up), at(place, down)

    barrier = pltpu.get_barrier_semaphore()
    partners = sides + [north_id, south_id] + peers
    for partner in partners:
        pl.semaphore_signal(barrier, inc=1, device_id=partner, device_id_type=MESH)

    copies = [
        pltpu.make_async_copy(control_hbm, control, local_sem.at[0]),
        pltpu.make_async_copy(coef_hbm, coef_in.at[pl.ds(0, 32)], local_sem.at[1]),
        pltpu.make_async_copy(coef_hbm, coef_in.at[pl.ds(32, 32)], local_sem.at[2]),
        pltpu.make_async_copy(eof_hbm, eof, local_sem.at[3]),
    ]
    for copy in copies:
        copy.start()
    levels = panel.shape[1] // count_z
    mine = pl.ds(pl.multiple_of(gz * levels, levels), levels)
    own_panel = pltpu.make_async_copy(
        panels_hbm.at[:, :, pl.ds(pl.multiple_of(gz * COLS, COLS), COLS)],
        panel.at[:, mine, :],
        local_sem.at[4],
    )
    own_panel.start()

    lane = lax.broadcasted_iota(jnp.int32, (8, COLS), 1)
    first_half = (lane & (SLOT - 1)) < HALF
    sub8 = lax.broadcasted_iota(jnp.int32, (8, COLS), 0)
    slots = [(lane >= SLOT * y) & (lane < SLOT * (y + 1)) for y in range(ROWS)]

    def slotted(edges, y, blocks):
        for g, block in enumerate(blocks):
            shifted = pltpu.roll(block, SLOT * y + HALF, 1)
            edges[g] = shifted if edges[g] is None else jnp.where(slots[y], shifted, edges[g])

    def pack_edges(edges, edge):
        for pair in range(0, len(edges), 2):
            one = edges[pair]
            two = edges[pair + 1] if pair + 1 < len(edges) else one
            easting = jnp.where(first_half, one, pltpu.roll(two, HALF, 1))
            westing = jnp.where(first_half, pltpu.roll(one, COLS - HALF, 1), two)
            edge[0, pair // 2] = easting.astype(jnp.bfloat16)
            edge[1, pair // 2] = westing.astype(jnp.bfloat16)

    for copy in copies[:3]:
        copy.wait()
    edges = [None] * (GROUPS + 1)
    for y in range(ROWS):
        fields = control[pl.ds(y, PLANES, stride=ROWS), :]
        entries = coef_in[pl.ds(y, 8, stride=ROWS), :]
        high = entries.astype(jnp.bfloat16).astype(jnp.float32)
        blocks = [jnp.where(sub8 < 4, high, entries - high)]
        blocks += [fields[8 * g : 8 * g + 8] for g in range(GROUPS)]
        for g, block in enumerate(blocks[1:]):
            tile_a[g, y] = block.astype(jnp.bfloat16)
        if y % 2 == 0:
            even, even_high = entries, high
        else:
            both = jnp.where(sub8 < 4, even, entries)
            tile_c[1 + y // 2] = both.astype(jnp.bfloat16)
            if y in (1, ROWS - 1):
                left = both - jnp.where(sub8 < 4, even_high, high)
                tile_c[0 if y == 1 else 1 + ROWS // 2] = left.astype(jnp.bfloat16)
        slotted(edges, y, blocks)
    pack_edges(edges, edge_a)

    def exchange(first, chunks, tile, edge, north, south, side, extra=()):
        moves = [(edge.at[k % 2], side.at[k], sides[k]) for k in range(6)]
        moves += extra
        for a, b in chunks:
            groups = pl.ds(a, b - a)
            moves.append((tile.at[groups, pl.ds(ROWS - DEPTH, DEPTH)], south.at[groups], north_id))
            moves.append((tile.at[groups, pl.ds(0, DEPTH)], north.at[groups], south_id))
        return [
            pltpu.make_async_remote_copy(
                src_ref=source,
                dst_ref=target,
                send_sem=send_sem.at[first + k],
                recv_sem=recv_sem.at[first + k],
                device_id=device,
                device_id_type=MESH,
            )
            for k, (source, target, device) in enumerate(moves)
        ]

    pl.semaphore_wait(barrier, len(partners))
    extra = [
        (tile_c.at[pl.ds(1 + (ROWS - DEPTH) // 2, DEPTH // 2 + 1)], south_c, north_id),
        (tile_c.at[pl.ds(0, DEPTH // 2 + 1)], north_c, south_id),
    ]
    halo_a = exchange(0, CHUNKS_A, tile_a, edge_a, north_a, south_a, side_a, extra)
    for copy in halo_a:
        copy.start()
    sent_panels = []
    for d in range(1, count_z):
        peer = lax.rem(gz + d, count_z)
        copy = pltpu.make_async_remote_copy(
            src_ref=panels_hbm.at[:, :, pl.ds(pl.multiple_of(peer * COLS, COLS), COLS)],
            dst_ref=panel.at[:, mine, :],
            send_sem=send_sem.at[33 + d],
            recv_sem=recv_sem.at[33 + d],
            device_id=peers[d - 1],
            device_id_type=MESH,
        )
        copy.start()
        sent_panels.append(copy)

    def put_coef(row, start, entries):
        for k in range(4):
            scale = TIME_STEP if k == 3 else 1.0
            entry = scale * entries[k : k + 1]
            coef[row, k, :, start : start + COLS] = jnp.broadcast_to(entry, (8, COLS))
            coef_rows[STRIDE * k + row : STRIDE * k + row + 1, start : start + COLS] = entry

    for y in range(ROWS):
        fields = control[pl.ds(y, PLANES, stride=ROWS), :]
        for g in range(GROUPS):
            grid[g, DEPTH + y, :, 0:COLS] = fields[8 * g : 8 * g + 8]
        put_coef(DEPTH + y, 0, coef_in[pl.ds(y, 8, stride=ROWS), :])

    turned[...] = jnp.zeros_like(turned)
    flux[...] = jnp.zeros_like(flux)
    for k in range(4):
        first = STRIDE * k + EXT
        coef_rows[first : STRIDE * (k + 1), :] = jnp.zeros((STRIDE - EXT, 2 * COLS), jnp.float32)
    coef_rows[4 * STRIDE :, :] = jnp.zeros((COLS - 4 * STRIDE, 2 * COLS), jnp.float32)

    copies[3].wait()
    count_e, count_f, count_l = eof.shape
    for e in range(count_e):
        block = eof[e].astype(jnp.float32)
        for f in range(count_f):
            basis[f * count_e + e : f * count_e + e + 1, :] = block[f : f + 1]
    plane = lax.broadcasted_iota(jnp.int32, (PLANES, 512), 0)
    field_of = jnp.zeros_like(plane)
    for f in range(1, count_f):
        field_of = field_of + jnp.where(plane >= f * count_e, 1, 0)
    spot = lax.broadcasted_iota(jnp.int32, (PLANES, 512), 1)
    same_field = field_of == (lax.shift_right_logical(spot, 5) & 3)
    level_row = lax.broadcasted_iota(jnp.int32, (count_l, 512), 0)
    level_spot = lax.broadcasted_iota(jnp.int32, (count_l, 512), 1)
    level_of = 4 * lax.shift_right_logical(level_spot, 7) + (lax.shift_right_logical(level_spot, 3) & 3)
    repeat = jnp.where(level_row == level_of, 1.0, 0.0).astype(jnp.bfloat16)
    spread = jnp.dot(basis[...].astype(jnp.bfloat16), repeat, preferred_element_type=jnp.float32)
    spread = jnp.where(same_field, spread, 0.0)
    for pair in range(ROWS // 2):
        both = [jnp.where((spot & 7) == 2 * pair + k, spread, 0.0) for k in range(2)]
        weight[pl.ds(2 * PLANES * pair, 2 * PLANES), :] = jnp.concatenate(both, axis=0).astype(jnp.bfloat16)

    keep_north = jnp.where(gy < count_y - 1, 1.0, 0.0).astype(jnp.float32)
    keep_south = jnp.where(gy > 0, 1.0, 0.0).astype(jnp.float32)
    ranges = (
        (DEPTH, 0, 0, ROWS, None),
        (0, 2, ROWS - DEPTH, DEPTH, keep_south),
        (DEPTH + ROWS, 4, 0, DEPTH, keep_north),
    )

    def edge_pack(side, group, k, keep):
        from_west = side[k, group // 2].astype(jnp.float32)
        from_east = side[k + 1, group // 2].astype(jnp.float32)
        if group % 2 == 0:
            pack = jnp.where(first_half, from_west, pltpu.roll(from_east, HALF, 1))
        else:
            pack = jnp.where(first_half, pltpu.roll(from_west, COLS - HALF, 1), from_east)
        return pack if keep is None else pack * keep

    def edge_rows(side, group):
        for start, k, slot, count, keep in ranges:
            pack = edge_pack(side, group, k, keep)
            for y in range(count):
                yield start + y, pltpu.roll(pack, COLS - HALF - SLOT * (y + slot), 1)

    def halo_rows(north, south, group):
        for y in range(DEPTH):
            yield y, south[group, y].astype(jnp.float32) * keep_south
            yield DEPTH + ROWS + y, north[group, y].astype(jnp.float32) * keep_north

    def joined(parts):
        return parts + pltpu.roll(parts, 4, 0)

    for copy in halo_a[:8]:
        copy.wait_recv()
    for row, block in edge_rows(side_a, 0):
        put_coef(row, COLS, joined(block))
    for half in range(DEPTH // 2):
        lower = south_c[half].astype(jnp.float32)
        upper = north_c[1 + half].astype(jnp.float32)
        if half == DEPTH // 2 - 1:
            lower = lower + south_c[half + 1].astype(jnp.float32)
        if half == 0:
            upper = upper + north_c[0].astype(jnp.float32)
        lower, upper = lower * keep_south, upper * keep_north
        for k in range(2):
            put_coef(2 * half + k, 0, lower[4 * k : 4 * k + 4])
            put_coef(DEPTH + ROWS + 2 * half + k, 0, upper[4 * k : 4 * k + 4])
    for g in range(GROUPS):
        for row, block in edge_rows(side_a, g + 1):
            grid[g, row, :, COLS:] = block
    for i, (a, b) in enumerate(CHUNKS_A):
        for copy in halo_a[8 + 2 * i : 10 + 2 * i]:
            copy.wait_recv()
        for g in range(a, b):
            for row, block in halo_rows(north_a, south_a, g):
                grid[g, row, :, 0:COLS] = block

        def step_a(g, carry):
            adjoint_steps(grid, coef, g)
            return carry

        lax.fori_loop(a, b, step_a, 0)


    pick_row = lax.broadcasted_iota(jnp.int32, (COLS, LINES * COLS), 0)
    pick_lane = lax.broadcasted_iota(jnp.int32, (COLS, LINES * COLS), 1)
    line_of = lax.shift_right_logical(pick_lane, 7)
    pick_lane = pick_lane & (COLS - 1)
    block_of = jnp.where(pick_lane >= PLANES, 1, 0) + jnp.where(pick_lane >= 2 * PLANES, 1, 0)
    wanted = jnp.where(pick_lane < 3 * PLANES, line_of + LINES * block_of, 2 * COLS)
    own, beyond = coef_rows[:, 0:COLS].T, coef_rows[:, COLS:].T
    rest = jnp.concatenate([beyond[COLS - 8 :], own, beyond[0:8]], axis=0)
    parts = []
    for _ in range(3):
        parts.append(rest.astype(jnp.bfloat16))
        rest = rest - parts[-1].astype(jnp.float32)
    left = jnp.concatenate(parts, axis=1)
    for k in range(4):
        ones = jnp.where(pick_row - STRIDE * k == wanted, 1.0, 0.0).astype(jnp.bfloat16)
        turn = jnp.dot(left, jnp.concatenate([ones] * 3, axis=0), preferred_element_type=jnp.float32)
        for g in range(LINES):
            coef_t[k, g] = turn[:, g * COLS : (g + 1) * COLS]

    own_panel.wait()
    for copy in sent_panels:
        copy.wait_recv()
    members = panel.shape[0]
    for m in range(0, members, 2):
        pair = jnp.concatenate([panel[m], panel[m + 1]], axis=1)
        projected[:, m * COLS : (m + 2) * COLS] = jnp.dot(
            weight[...], pair, preferred_element_type=jnp.float32
        )

    edges = [None] * GROUPS
    for y in range(ROWS):
        factor = jnp.concatenate([grid[g, DEPTH + y, :, 0:COLS] for g in range(GROUPS)], axis=0)
        row = None
        for m in range(members):
            term = projected[y * PLANES : (y + 1) * PLANES, m * COLS : (m + 1) * COLS]
            score = jnp.sum(term * factor, axis=0, keepdims=True) * (1.0 / (members - 1))
            row = term * score if row is None else row + term * score
        blocks = [row[8 * g : 8 * g + 8] for g in range(GROUPS)]
        for g, block in enumerate(blocks):
            own_b[g, y] = block
            tile_b[g, y] = block.astype(jnp.bfloat16)
        slotted(edges, y, blocks)
    pack_edges(edges, edge_b)

    first_b = len(halo_a)
    halo_b = exchange(first_b, CHUNKS_B, tile_b, edge_b, north_b, south_b, side_b)
    for copy in halo_b:
        copy.start()
    for copy in halo_b[:6]:
        copy.wait_recv()
    lanes = lax.broadcasted_iota(jnp.int32, (8, COLS), 1)
    spare = jnp.zeros((COLS - 3 * PLANES, COLS), jnp.float32)
    packs = [edge_pack(side_b, g, k, keep) for k, keep in ((2, keep_south), (0, None), (4, keep_north)) for g in range(GROUPS)]
    packs = jnp.concatenate(packs + [spare], axis=0).T
    for east_side in range(2):
        place_at = pl.ds(east_side * (TALL - 8), 8)

        def piece(y):
            first = SLOT * y + HALF * east_side
            return packs[first : first + 8]

        for g in range(DEPTH):
            middle = jnp.where(lanes < 2 * PLANES, piece(1 + g), piece(g))
            turned[g, place_at] = jnp.where(lanes < PLANES, piece(2 + g), middle)
        turned[DEPTH, place_at] = jnp.where(lanes < PLANES, pltpu.roll(piece(0), COLS - PLANES, 1), piece(ROWS - 1))
    main = pl.ds(8, COLS)
    ends = [own_b[g, y] for y in (0, ROWS - 1) for g in range(GROUPS)]
    ends.append(jnp.zeros((COLS - 2 * PLANES, COLS), jnp.float32))
    turned[DEPTH, main] = jnp.concatenate(ends, axis=0).T
    for copy in halo_b[6:]:
        copy.wait_recv()
    for line in range(DEPTH):
        stack = [south_b[g, line].astype(jnp.float32) * keep_south for g in range(GROUPS)]
        stack += [own_b[g, 1 + line] for g in range(GROUPS)]
        stack += [north_b[g, line].astype(jnp.float32) * keep_north for g in range(GROUPS)]
        turned[line, main] = jnp.concatenate(stack + [spare], axis=0).T
    forward_steps(turned, flux, coef_t)
    for line in range(LINES):
        back = turned[line, main].T
        if line < DEPTH:
            out_ref[pl.ds(1 + line, PLANES, stride=ROWS), :] = back[PLANES : 2 * PLANES]
        else:
            out_ref[pl.ds(0, PLANES, stride=ROWS), :] = back[0:PLANES]
            out_ref[pl.ds(ROWS - 1, PLANES, stride=ROWS), :] = back[PLANES : 2 * PLANES]
    for copy in halo_a + sent_panels + halo_b:
        copy.wait_send()


def solution(mesh):
    sizes = tuple(mesh.shape[name] for name in ("gx", "gy", "gz"))

    def per_device(panels, eof_basis, control, coefficients):
        members, fields, levels, rows, columns = panels.shape
        eof_count = eof_basis.shape[2]
        deep = fields * levels * rows
        f32, bf16 = jnp.float32, jnp.bfloat16
        anywhere = pl.BlockSpec(memory_space=pl.ANY)
        wide = GROUPS + 1
        pairs_a, pairs_b = wide // 2, (GROUPS + 1) // 2
        out = pl.pallas_call(
            functools.partial(kernel, sizes),
            out_shape=jax.ShapeDtypeStruct((PLANES * ROWS, COLS), f32),
            in_specs=[anywhere] * 4,
            out_specs=pl.BlockSpec(memory_space=pltpu.VMEM),
            scratch_shapes=[
                pltpu.VMEM((PLANES * ROWS, COLS), f32),
                pltpu.VMEM((8 * ROWS, COLS), f32),
                pltpu.VMEM((eof_count, fields, levels * sizes[2]), bf16),
                pltpu.VMEM((PLANES, levels * sizes[2]), f32),
                pltpu.VMEM((members, deep * sizes[2], COLS), bf16),
                pltpu.VMEM((PLANES * ROWS, deep * sizes[2]), bf16),
                pltpu.VMEM((PLANES * ROWS, members * COLS), f32),
                pltpu.VMEM((GROUPS, EXT, 8, 2 * COLS), f32),
                pltpu.VMEM((EXT, 4, 8, 2 * COLS), f32),
                pltpu.VMEM((ROWS // 2 + 2, 8, COLS), bf16),
                pltpu.VMEM((DEPTH // 2 + 1, 8, COLS), bf16),
                pltpu.VMEM((DEPTH // 2 + 1, 8, COLS), bf16),
                pltpu.VMEM((GROUPS, ROWS, 8, COLS), bf16),
                pltpu.VMEM((2, pairs_a, 8, COLS), bf16),
                pltpu.VMEM((GROUPS, DEPTH, 8, COLS), bf16),
                pltpu.VMEM((GROUPS, DEPTH, 8, COLS), bf16),
                pltpu.VMEM((6, pairs_a, 8, COLS), bf16),
                pltpu.VMEM((GROUPS, ROWS, 8, COLS), bf16),
                pltpu.VMEM((2, pairs_b, 8, COLS), bf16),
                pltpu.VMEM((GROUPS, DEPTH, 8, COLS), bf16),
                pltpu.VMEM((GROUPS, DEPTH, 8, COLS), bf16),
                pltpu.VMEM((6, pairs_b, 8, COLS), bf16),
                pltpu.VMEM((GROUPS, ROWS, 8, COLS), f32),
                pltpu.VMEM((LINES, TALL + 8, COLS), f32),
                pltpu.VMEM((LINES, TALL + 8, COLS), f32),
                pltpu.VMEM((COLS, 2 * COLS), f32),
                pltpu.VMEM((4, LINES, TALL, COLS), f32),
                pltpu.SemaphoreType.DMA((5,)),
                pltpu.SemaphoreType.DMA((44,)),
                pltpu.SemaphoreType.DMA((44,)),
            ],
            compiler_params=pltpu.CompilerParams(
                collective_id=0, has_side_effects=True, vmem_limit_bytes=63 * 1024 * 1024
            ),
            name="covariance",
        )(
            panels.reshape(members, deep, columns),
            eof_basis.transpose(2, 0, 1),
            control.reshape(-1, COLS),
            coefficients.reshape(-1, COLS),
        )
        return out.reshape(control.shape)

    in_specs = (
        P(None, None, "gz", "gy", "gx"),
        P(),
        P(None, None, "gy", ("gx", "gz")),
        P(None, "gy", ("gx", "gz")),
    )
    return jax.shard_map(
        per_device,
        mesh=mesh,
        in_specs=in_specs,
        out_specs=P(None, None, "gy", ("gx", "gz")),
        check_vma=False,
    )
```

```python
import functools

import jax
import jax.numpy as jnp
from jax import lax
from jax.experimental import pallas as pl
from jax.experimental.pallas import tpu as pltpu
from jax.sharding import PartitionSpec as P

STEPS = 6
TIME_STEP = 0.09
ROWS = 8
COLS = 128
DEPTH = STEPS
EXT = ROWS + 2 * DEPTH
SLOT = COLS // ROWS
HALF = SLOT // 2
PLANES = 40
GROUPS = PLANES // 8
LAG = 2
LINES = 7
TALL = COLS + 16
STRIDE = 24
CHUNKS_A = ((0, 1), (1, 3), (3, 5))
CHUNKS_B = ((0, GROUPS),)
MESH = pl.DeviceIdType.MESH


def adjoint_steps(grid, coef, group):
    level = [{} for _ in range(STEPS + 1)]
    below = [None] * STEPS
    weighted = [{} for _ in range(STEPS)]

    def source(k, r):
        if r not in weighted[k]:
            weighted[k][r] = coef[r, 3] * level[k][r]
        return weighted[k][r]

    def update(k, r):
        here, above = source(k, r), source(k, r + 1)
        east = pltpu.roll(here, 2 * COLS - 1, 1) - here
        north = above - here
        kxy = coef[r, 1]
        flux_north = kxy * east + coef[r, 2] * north
        if r > k:
            flux_east = coef[r, 0] * east + kxy * north
            div = (flux_east - pltpu.roll(flux_east, 1, 1)) + (flux_north - below[k])
            old = level[k][r]
            new = old + div
            if k == STEPS - 1:
                grid[group, r] = new
            else:
                level[k + 1][r] = new
        below[k] = flux_north

    level[0][0] = grid[group, 0]
    for top in range(1, EXT + LAG * STEPS):
        if top < EXT:
            level[0][top] = grid[group, top]
        for k in range(STEPS):
            r = top - 1 - LAG * k
            if k <= r <= EXT - 2 - k:
                update(k, r)


def forward_steps(turned, flux, coef_t):
    part = TALL // 3

    def one_step(_, carry):
        for c in range(3):
            rows = pl.ds(part * c, part)
            ahead = pl.ds(part * c + 1, part)
            behind = pl.ds(8 + part * c - 1, part)
            stored = pl.ds(8 + part * c, part)

            def flux_of(g, here, above):
                east = turned[g, ahead] - here
                north = above - here
                kxy = coef_t[1, g, rows]
                return coef_t[0, g, rows] * east + kxy * north, kxy * east + coef_t[2, g, rows] * north

            last = turned[LINES - 1, rows]
            after_last = pltpu.roll(turned[0, rows], COLS - PLANES, 1)
            last_east, last_north = flux_of(LINES - 1, last, after_last)
            below = pltpu.roll(last_north, PLANES, 1)
            here = turned[0, rows]
            for g in range(LINES):
                if g < LINES - 1:
                    above = turned[g + 1, rows]
                    flux_east, flux_north = flux_of(g, here, above)
                else:
                    flux_east, flux_north = last_east, last_north
                flux[g, stored] = flux_east
                turned[g, rows] = here + coef_t[3, g, rows] * (
                    (flux_east - flux[g, behind]) + (flux_north - below)
                )
                below = flux_north
                here = above
        return carry

    lax.fori_loop(0, STEPS, one_step, 0)


def kernel(
    sizes,
    panels_hbm,
    eof_hbm,
    control_hbm,
    coef_hbm,
    out_ref,
    control,
    coef_in,
    eof,
    basis,
    panel,
    weight,
    projected,
    grid,
    coef,
    tile_c,
    north_c,
    south_c,
    tile_a,
    edge_a,
    north_a,
    south_a,
    side_a,
    tile_b,
    edge_b,
    north_b,
    south_b,
    side_b,
    own_b,
    turned,
    flux,
    coef_rows,
    coef_t,
    local_sem,
    send_sem,
    recv_sem,
):
    count_x, count_y, count_z = sizes
    gx, gy, gz = lax.axis_index("gx"), lax.axis_index("gy"), lax.axis_index("gz")
    place = gx * count_z + gz
    total = count_x * count_z
    east = lax.rem(place + 1, total)
    west = lax.rem(place + total - 1, total)
    up = lax.rem(gy + 1, count_y)
    down = lax.rem(gy + count_y - 1, count_y)

    def at(column, row):
        return (column // count_z, row, lax.rem(column, count_z))

    sides = [at(east, gy), at(west, gy), at(east, up), at(west, up), at(east, down), at(west, down)]
    peers = [(gx, gy, lax.rem(gz + d, count_z)) for d in range(1, count_z)]
    north_id, south_id = at(place, up), at(place, down)

    barrier = pltpu.get_barrier_semaphore()
    partners = sides + [north_id, south_id] + peers
    for partner in partners:
        pl.semaphore_signal(barrier, inc=1, device_id=partner, device_id_type=MESH)

    copies = [
        pltpu.make_async_copy(control_hbm, control, local_sem.at[0]),
        pltpu.make_async_copy(coef_hbm, coef_in.at[pl.ds(0, 32)], local_sem.at[1]),
        pltpu.make_async_copy(coef_hbm, coef_in.at[pl.ds(32, 32)], local_sem.at[2]),
        pltpu.make_async_copy(eof_hbm, eof, local_sem.at[3]),
    ]
    for copy in copies:
        copy.start()
    levels = panel.shape[1] // count_z
    mine = pl.ds(pl.multiple_of(gz * levels, levels), levels)
    own_panel = pltpu.make_async_copy(
        panels_hbm.at[:, :, pl.ds(pl.multiple_of(gz * COLS, COLS), COLS)],
        panel.at[:, mine, :],
        local_sem.at[4],
    )
    own_panel.start()

    lane = lax.broadcasted_iota(jnp.int32, (8, COLS), 1)
    first_half = (lane & (SLOT - 1)) < HALF
    sub8 = lax.broadcasted_iota(jnp.int32, (8, COLS), 0)
    slots = [(lane >= SLOT * y) & (lane < SLOT * (y + 1)) for y in range(ROWS)]

    def slotted(edges, y, blocks):
        for g, block in enumerate(blocks):
            shifted = pltpu.roll(block, SLOT * y + HALF, 1)
            edges[g] = shifted if edges[g] is None else jnp.where(slots[y], shifted, edges[g])

    def pack_edges(edges, edge):
        for pair in range(0, len(edges), 2):
            one = edges[pair]
            two = edges[pair + 1] if pair + 1 < len(edges) else one
            easting = jnp.where(first_half, one, pltpu.roll(two, HALF, 1))
            westing = jnp.where(first_half, pltpu.roll(one, COLS - HALF, 1), two)
            edge[0, pair // 2] = easting.astype(jnp.bfloat16)
            edge[1, pair // 2] = westing.astype(jnp.bfloat16)

    members = panel.shape[0]
    sent_panels = []

    def send_panels(first, last, row, end):
        some = pl.ds(first, last - first)
        for d in range(1, count_z):
            peer = lax.rem(gz + d, count_z)
            spot = pl.ds(pl.multiple_of(gz * levels + row, 16), end - row)
            copy = pltpu.make_async_remote_copy(
                src_ref=panels_hbm.at[some, pl.ds(row, end - row), pl.ds(pl.multiple_of(peer * COLS, COLS), COLS)],
                dst_ref=panel.at[some, spot, :],
                send_sem=send_sem.at[33 + len(sent_panels)],
                recv_sem=recv_sem.at[33 + len(sent_panels)],
                device_id=peers[d - 1],
                device_id_type=MESH,
            )
            copy.start()
            sent_panels.append(copy)

    pl.semaphore_wait(barrier, len(partners))
    send_panels(0, 1, 0, 64)

    for copy in copies[:3]:
        copy.wait()
    edges = [None] * (GROUPS + 1)
    for y in range(ROWS):
        fields = control[pl.ds(y, PLANES, stride=ROWS), :]
        entries = coef_in[pl.ds(y, 8, stride=ROWS), :]
        high = entries.astype(jnp.bfloat16).astype(jnp.float32)
        blocks = [jnp.where(sub8 < 4, high, entries - high)]
        blocks += [fields[8 * g : 8 * g + 8] for g in range(GROUPS)]
        for g, block in enumerate(blocks[1:]):
            tile_a[g, y] = block.astype(jnp.bfloat16)
        if y % 2 == 0:
            even, even_high = entries, high
        else:
            both = jnp.where(sub8 < 4, even, entries)
            tile_c[1 + y // 2] = both.astype(jnp.bfloat16)
            if y in (1, ROWS - 1):
                left = both - jnp.where(sub8 < 4, even_high, high)
                tile_c[0 if y == 1 else 1 + ROWS // 2] = left.astype(jnp.bfloat16)
        slotted(edges, y, blocks)
    pack_edges(edges, edge_a)

    def exchange(first, chunks, tile, edge, north, south, side, extra=()):
        moves = [(edge.at[k % 2], side.at[k], sides[k]) for k in range(6)]
        moves += extra
        for a, b in chunks:
            groups = pl.ds(a, b - a)
            moves.append((tile.at[groups, pl.ds(ROWS - DEPTH, DEPTH)], south.at[groups], north_id))
            moves.append((tile.at[groups, pl.ds(0, DEPTH)], north.at[groups], south_id))
        return [
            pltpu.make_async_remote_copy(
                src_ref=source,
                dst_ref=target,
                send_sem=send_sem.at[first + k],
                recv_sem=recv_sem.at[first + k],
                device_id=device,
                device_id_type=MESH,
            )
            for k, (source, target, device) in enumerate(moves)
        ]

    extra = [
        (tile_c.at[pl.ds(1 + (ROWS - DEPTH) // 2, DEPTH // 2 + 1)], south_c, north_id),
        (tile_c.at[pl.ds(0, DEPTH // 2 + 1)], north_c, south_id),
    ]
    halo_a = exchange(0, CHUNKS_A, tile_a, edge_a, north_a, south_a, side_a, extra)
    for copy in halo_a:
        copy.start()
    send_panels(0, 1, 64, levels)
    send_panels(1, members, 0, levels)

    def put_coef(row, start, entries):
        for k in range(4):
            scale = TIME_STEP if k == 3 else 1.0
            entry = scale * entries[k : k + 1]
            coef[row, k, :, start : start + COLS] = jnp.broadcast_to(entry, (8, COLS))
            coef_rows[STRIDE * k + row : STRIDE * k + row + 1, start : start + COLS] = entry

    for y in range(ROWS):
        fields = control[pl.ds(y, PLANES, stride=ROWS), :]
        for g in range(GROUPS):
            grid[g, DEPTH + y, :, 0:COLS] = fields[8 * g : 8 * g + 8]
        put_coef(DEPTH + y, 0, coef_in[pl.ds(y, 8, stride=ROWS), :])

    turned[...] = jnp.zeros_like(turned)
    flux[...] = jnp.zeros_like(flux)
    for k in range(4):
        first = STRIDE * k + EXT
        coef_rows[first : STRIDE * (k + 1), :] = jnp.zeros((STRIDE - EXT, 2 * COLS), jnp.float32)
    coef_rows[4 * STRIDE :, :] = jnp.zeros((COLS - 4 * STRIDE, 2 * COLS), jnp.float32)

    copies[3].wait()
    count_e, count_f, count_l = eof.shape
    for e in range(count_e):
        block = eof[e].astype(jnp.float32)
        for f in range(count_f):
            basis[f * count_e + e : f * count_e + e + 1, :] = block[f : f + 1]
    plane = lax.broadcasted_iota(jnp.int32, (PLANES, 512), 0)
    field_of = jnp.zeros_like(plane)
    for f in range(1, count_f):
        field_of = field_of + jnp.where(plane >= f * count_e, 1, 0)
    spot = lax.broadcasted_iota(jnp.int32, (PLANES, 512), 1)
    same_field = field_of == (lax.shift_right_logical(spot, 5) & 3)
    level_row = lax.broadcasted_iota(jnp.int32, (count_l, 512), 0)
    level_spot = lax.broadcasted_iota(jnp.int32, (count_l, 512), 1)
    level_of = 4 * lax.shift_right_logical(level_spot, 7) + (lax.shift_right_logical(level_spot, 3) & 3)
    repeat = jnp.where(level_row == level_of, 1.0, 0.0).astype(jnp.bfloat16)
    spread = jnp.dot(basis[...].astype(jnp.bfloat16), repeat, preferred_element_type=jnp.float32)
    spread = jnp.where(same_field, spread, 0.0)
    for pair in range(ROWS // 2):
        both = [jnp.where((spot & 7) == 2 * pair + k, spread, 0.0) for k in range(2)]
        weight[pl.ds(2 * PLANES * pair, 2 * PLANES), :] = jnp.concatenate(both, axis=0).astype(jnp.bfloat16)

    keep_north = jnp.where(gy < count_y - 1, 1.0, 0.0).astype(jnp.float32)
    keep_south = jnp.where(gy > 0, 1.0, 0.0).astype(jnp.float32)
    ranges = (
        (DEPTH, 0, 0, ROWS, None),
        (0, 2, ROWS - DEPTH, DEPTH, keep_south),
        (DEPTH + ROWS, 4, 0, DEPTH, keep_north),
    )

    def edge_pack(side, group, k, keep):
        from_west = side[k, group // 2].astype(jnp.float32)
        from_east = side[k + 1, group // 2].astype(jnp.float32)
        if group % 2 == 0:
            pack = jnp.where(first_half, from_west, pltpu.roll(from_east, HALF, 1))
        else:
            pack = jnp.where(first_half, pltpu.roll(from_west, COLS - HALF, 1), from_east)
        return pack if keep is None else pack * keep

    def edge_rows(side, group):
        for start, k, slot, count, keep in ranges:
            pack = edge_pack(side, group, k, keep)
            for y in range(count):
                yield start + y, pltpu.roll(pack, COLS - HALF - SLOT * (y + slot), 1)

    def halo_rows(north, south, group):
        for y in range(DEPTH):
            yield y, south[group, y].astype(jnp.float32) * keep_south
            yield DEPTH + ROWS + y, north[group, y].astype(jnp.float32) * keep_north

    def joined(parts):
        return parts + pltpu.roll(parts, 4, 0)

    for copy in halo_a[:8]:
        copy.wait_recv()
    for row, block in edge_rows(side_a, 0):
        put_coef(row, COLS, joined(block))
    for half in range(DEPTH // 2):
        lower = south_c[half].astype(jnp.float32)
        upper = north_c[1 + half].astype(jnp.float32)
        if half == DEPTH // 2 - 1:
            lower = lower + south_c[half + 1].astype(jnp.float32)
        if half == 0:
            upper = upper + north_c[0].astype(jnp.float32)
        lower, upper = lower * keep_south, upper * keep_north
        for k in range(2):
            put_coef(2 * half + k, 0, lower[4 * k : 4 * k + 4])
            put_coef(DEPTH + ROWS + 2 * half + k, 0, upper[4 * k : 4 * k + 4])
    for g in range(GROUPS):
        for row, block in edge_rows(side_a, g + 1):
            grid[g, row, :, COLS:] = block
    for i, (a, b) in enumerate(CHUNKS_A):
        for copy in halo_a[8 + 2 * i : 10 + 2 * i]:
            copy.wait_recv()
        for g in range(a, b):
            for row, block in halo_rows(north_a, south_a, g):
                grid[g, row, :, 0:COLS] = block

        def step_a(g, carry):
            adjoint_steps(grid, coef, g)
            return carry

        lax.fori_loop(a, b, step_a, 0)


    pick_row = lax.broadcasted_iota(jnp.int32, (COLS, LINES * COLS), 0)
    pick_lane = lax.broadcasted_iota(jnp.int32, (COLS, LINES * COLS), 1)
    line_of = lax.shift_right_logical(pick_lane, 7)
    pick_lane = pick_lane & (COLS - 1)
    block_of = jnp.where(pick_lane >= PLANES, 1, 0) + jnp.where(pick_lane >= 2 * PLANES, 1, 0)
    wanted = jnp.where(pick_lane < 3 * PLANES, line_of + LINES * block_of, 2 * COLS)
    own, beyond = coef_rows[:, 0:COLS].T, coef_rows[:, COLS:].T
    rest = jnp.concatenate([beyond[COLS - 8 :], own, beyond[0:8]], axis=0)
    parts = []
    for _ in range(3):
        parts.append(rest.astype(jnp.bfloat16))
        rest = rest - parts[-1].astype(jnp.float32)
    left = jnp.concatenate(parts, axis=1)
    for k in range(4):
        ones = jnp.where(pick_row - STRIDE * k == wanted, 1.0, 0.0).astype(jnp.bfloat16)
        turn = jnp.dot(left, jnp.concatenate([ones] * 3, axis=0), preferred_element_type=jnp.float32)
        for g in range(LINES):
            coef_t[k, g] = turn[:, g * COLS : (g + 1) * COLS]

    own_panel.wait()
    for copy in sent_panels:
        copy.wait_recv()
    for m in range(0, members, 2):
        pair = jnp.concatenate([panel[m], panel[m + 1]], axis=1)
        projected[:, m * COLS : (m + 2) * COLS] = jnp.dot(
            weight[...], pair, preferred_element_type=jnp.float32
        )

    edges = [None] * GROUPS
    for y in range(ROWS):
        factor = jnp.concatenate([grid[g, DEPTH + y, :, 0:COLS] for g in range(GROUPS)], axis=0)
        row = None
        for m in range(members):
            term = projected[y * PLANES : (y + 1) * PLANES, m * COLS : (m + 1) * COLS]
            score = jnp.sum(term * factor, axis=0, keepdims=True) * (1.0 / (members - 1))
            row = term * score if row is None else row + term * score
        blocks = [row[8 * g : 8 * g + 8] for g in range(GROUPS)]
        for g, block in enumerate(blocks):
            own_b[g, y] = block
            tile_b[g, y] = block.astype(jnp.bfloat16)
        slotted(edges, y, blocks)
    pack_edges(edges, edge_b)

    first_b = len(halo_a)
    halo_b = exchange(first_b, CHUNKS_B, tile_b, edge_b, north_b, south_b, side_b)
    for copy in halo_b:
        copy.start()
    for copy in halo_b[:6]:
        copy.wait_recv()
    lanes = lax.broadcasted_iota(jnp.int32, (8, COLS), 1)
    spare = jnp.zeros((COLS - 3 * PLANES, COLS), jnp.float32)
    packs = [edge_pack(side_b, g, k, keep) for k, keep in ((2, keep_south), (0, None), (4, keep_north)) for g in range(GROUPS)]
    packs = jnp.concatenate(packs + [spare], axis=0).T
    for east_side in range(2):
        place_at = pl.ds(east_side * (TALL - 8), 8)

        def piece(y):
            first = SLOT * y + HALF * east_side
            return packs[first : first + 8]

        for g in range(DEPTH):
            middle = jnp.where(lanes < 2 * PLANES, piece(1 + g), piece(g))
            turned[g, place_at] = jnp.where(lanes < PLANES, piece(2 + g), middle)
        turned[DEPTH, place_at] = jnp.where(lanes < PLANES, pltpu.roll(piece(0), COLS - PLANES, 1), piece(ROWS - 1))
    main = pl.ds(8, COLS)
    ends = [own_b[g, y] for y in (0, ROWS - 1) for g in range(GROUPS)]
    ends.append(jnp.zeros((COLS - 2 * PLANES, COLS), jnp.float32))
    turned[DEPTH, main] = jnp.concatenate(ends, axis=0).T
    for copy in halo_b[6:]:
        copy.wait_recv()
    for line in range(DEPTH):
        stack = [south_b[g, line].astype(jnp.float32) * keep_south for g in range(GROUPS)]
        stack += [own_b[g, 1 + line] for g in range(GROUPS)]
        stack += [north_b[g, line].astype(jnp.float32) * keep_north for g in range(GROUPS)]
        turned[line, main] = jnp.concatenate(stack + [spare], axis=0).T
    forward_steps(turned, flux, coef_t)
    for line in range(LINES):
        back = turned[line, main].T
        if line < DEPTH:
            out_ref[pl.ds(1 + line, PLANES, stride=ROWS), :] = back[PLANES : 2 * PLANES]
        else:
            out_ref[pl.ds(0, PLANES, stride=ROWS), :] = back[0:PLANES]
            out_ref[pl.ds(ROWS - 1, PLANES, stride=ROWS), :] = back[PLANES : 2 * PLANES]
    for copy in halo_a + sent_panels + halo_b:
        copy.wait_send()


def solution(mesh):
    sizes = tuple(mesh.shape[name] for name in ("gx", "gy", "gz"))

    def per_device(panels, eof_basis, control, coefficients):
        members, fields, levels, rows, columns = panels.shape
        eof_count = eof_basis.shape[2]
        deep = fields * levels * rows
        f32, bf16 = jnp.float32, jnp.bfloat16
        anywhere = pl.BlockSpec(memory_space=pl.ANY)
        wide = GROUPS + 1
        pairs_a, pairs_b = wide // 2, (GROUPS + 1) // 2
        out = pl.pallas_call(
            functools.partial(kernel, sizes),
            out_shape=jax.ShapeDtypeStruct((PLANES * ROWS, COLS), f32),
            in_specs=[anywhere] * 4,
            out_specs=pl.BlockSpec(memory_space=pltpu.VMEM),
            scratch_shapes=[
                pltpu.VMEM((PLANES * ROWS, COLS), f32),
                pltpu.VMEM((8 * ROWS, COLS), f32),
                pltpu.VMEM((eof_count, fields, levels * sizes[2]), bf16),
                pltpu.VMEM((PLANES, levels * sizes[2]), f32),
                pltpu.VMEM((members, deep * sizes[2], COLS), bf16),
                pltpu.VMEM((PLANES * ROWS, deep * sizes[2]), bf16),
                pltpu.VMEM((PLANES * ROWS, members * COLS), f32),
                pltpu.VMEM((GROUPS, EXT, 8, 2 * COLS), f32),
                pltpu.VMEM((EXT, 4, 8, 2 * COLS), f32),
                pltpu.VMEM((ROWS // 2 + 2, 8, COLS), bf16),
                pltpu.VMEM((DEPTH // 2 + 1, 8, COLS), bf16),
                pltpu.VMEM((DEPTH // 2 + 1, 8, COLS), bf16),
                pltpu.VMEM((GROUPS, ROWS, 8, COLS), bf16),
                pltpu.VMEM((2, pairs_a, 8, COLS), bf16),
                pltpu.VMEM((GROUPS, DEPTH, 8, COLS), bf16),
                pltpu.VMEM((GROUPS, DEPTH, 8, COLS), bf16),
                pltpu.VMEM((6, pairs_a, 8, COLS), bf16),
                pltpu.VMEM((GROUPS, ROWS, 8, COLS), bf16),
                pltpu.VMEM((2, pairs_b, 8, COLS), bf16),
                pltpu.VMEM((GROUPS, DEPTH, 8, COLS), bf16),
                pltpu.VMEM((GROUPS, DEPTH, 8, COLS), bf16),
                pltpu.VMEM((6, pairs_b, 8, COLS), bf16),
                pltpu.VMEM((GROUPS, ROWS, 8, COLS), f32),
                pltpu.VMEM((LINES, TALL + 8, COLS), f32),
                pltpu.VMEM((LINES, TALL + 8, COLS), f32),
                pltpu.VMEM((COLS, 2 * COLS), f32),
                pltpu.VMEM((4, LINES, TALL, COLS), f32),
                pltpu.SemaphoreType.DMA((5,)),
                pltpu.SemaphoreType.DMA((44,)),
                pltpu.SemaphoreType.DMA((44,)),
            ],
            compiler_params=pltpu.CompilerParams(
                collective_id=0, has_side_effects=True, vmem_limit_bytes=63 * 1024 * 1024
            ),
            name="covariance",
        )(
            panels.reshape(members, deep, columns),
            eof_basis.transpose(2, 0, 1),
            control.reshape(-1, COLS),
            coefficients.reshape(-1, COLS),
        )
        return out.reshape(control.shape)

    in_specs = (
        P(None, None, "gz", "gy", "gx"),
        P(),
        P(None, None, "gy", ("gx", "gz")),
        P(None, "gy", ("gx", "gz")),
    )
    return jax.shard_map(
        per_device,
        mesh=mesh,
        in_specs=in_specs,
        out_specs=P(None, None, "gy", ("gx", "gz")),
        check_vma=False,
    )
```

```python
import functools

import jax
import jax.numpy as jnp
from jax import lax
from jax.experimental import pallas as pl
from jax.experimental.pallas import tpu as pltpu
from jax.sharding import PartitionSpec as P

STEPS = 6
TIME_STEP = 0.09
ROWS = 8
COLS = 128
DEPTH = STEPS
EXT = ROWS + 2 * DEPTH
SLOT = COLS // ROWS
HALF = SLOT // 2
PLANES = 40
GROUPS = PLANES // 8
LAG = 2
LINES = 7
TALL = COLS + 16
STRIDE = 24
CHUNKS_A = ((0, 1), (1, 3), (3, 5))
CHUNKS_B = ((0, GROUPS),)
MESH = pl.DeviceIdType.MESH


def adjoint_steps(grid, coef, group):
    level = [{} for _ in range(STEPS + 1)]
    below = [None] * STEPS
    weighted = [{} for _ in range(STEPS)]

    def source(k, r):
        if r not in weighted[k]:
            weighted[k][r] = coef[r, 3] * level[k][r]
        return weighted[k][r]

    def update(k, r):
        here, above = source(k, r), source(k, r + 1)
        east = pltpu.roll(here, 2 * COLS - 1, 1) - here
        north = above - here
        kxy = coef[r, 1]
        flux_north = kxy * east + coef[r, 2] * north
        if r > k:
            flux_east = coef[r, 0] * east + kxy * north
            div = (flux_east - pltpu.roll(flux_east, 1, 1)) + (flux_north - below[k])
            old = level[k][r]
            new = old + div
            if k == STEPS - 1:
                grid[group, r] = new
            else:
                level[k + 1][r] = new
        below[k] = flux_north

    level[0][0] = grid[group, 0]
    for top in range(1, EXT + LAG * STEPS):
        if top < EXT:
            level[0][top] = grid[group, top]
        for k in range(STEPS):
            r = top - 1 - LAG * k
            if k <= r <= EXT - 2 - k:
                update(k, r)


def forward_steps(turned, flux, coef_t):
    part = TALL // 3

    def one_step(_, carry):
        for c in range(3):
            rows = pl.ds(part * c, part)
            ahead = pl.ds(part * c + 1, part)
            behind = pl.ds(8 + part * c - 1, part)
            stored = pl.ds(8 + part * c, part)

            def flux_of(g, here, above):
                east = turned[g, ahead] - here
                north = above - here
                kxy = coef_t[1, g, rows]
                return coef_t[0, g, rows] * east + kxy * north, kxy * east + coef_t[2, g, rows] * north

            last = turned[LINES - 1, rows]
            after_last = pltpu.roll(turned[0, rows], COLS - PLANES, 1)
            last_east, last_north = flux_of(LINES - 1, last, after_last)
            below = pltpu.roll(last_north, PLANES, 1)
            here = turned[0, rows]
            for g in range(LINES):
                if g < LINES - 1:
                    above = turned[g + 1, rows]
                    flux_east, flux_north = flux_of(g, here, above)
                else:
                    flux_east, flux_north = last_east, last_north
                flux[g, stored] = flux_east
                turned[g, rows] = here + coef_t[3, g, rows] * (
                    (flux_east - flux[g, behind]) + (flux_north - below)
                )
                below = flux_north
                here = above
        return carry

    lax.fori_loop(0, STEPS, one_step, 0)


def kernel(
    sizes,
    panels_hbm,
    eof_hbm,
    control_hbm,
    coef_hbm,
    out_ref,
    control,
    coef_in,
    eof,
    basis,
    panel,
    weight,
    projected,
    grid,
    coef,
    tile_c,
    north_c,
    south_c,
    tile_a,
    edge_a,
    north_a,
    south_a,
    side_a,
    tile_b,
    edge_b,
    north_b,
    south_b,
    side_b,
    own_b,
    turned,
    flux,
    coef_rows,
    coef_t,
    finished,
    local_sem,
    send_sem,
    recv_sem,
):
    count_x, count_y, count_z = sizes
    gx, gy, gz = lax.axis_index("gx"), lax.axis_index("gy"), lax.axis_index("gz")
    place = gx * count_z + gz
    total = count_x * count_z
    east = lax.rem(place + 1, total)
    west = lax.rem(place + total - 1, total)
    up = lax.rem(gy + 1, count_y)
    down = lax.rem(gy + count_y - 1, count_y)

    def at(column, row):
        return (column // count_z, row, lax.rem(column, count_z))

    sides = [at(east, gy), at(west, gy), at(east, up), at(west, up), at(east, down), at(west, down)]
    peers = [(gx, gy, lax.rem(gz + d, count_z)) for d in range(1, count_z)]
    north_id, south_id = at(place, up), at(place, down)

    barrier = pltpu.get_barrier_semaphore()
    partners = sides + [north_id, south_id] + peers
    for partner in partners:
        pl.semaphore_signal(barrier, inc=1, device_id=partner, device_id_type=MESH)

    copies = [
        pltpu.make_async_copy(control_hbm, control, local_sem.at[0]),
        pltpu.make_async_copy(coef_hbm, coef_in.at[pl.ds(0, 32)], local_sem.at[1]),
        pltpu.make_async_copy(coef_hbm, coef_in.at[pl.ds(32, 32)], local_sem.at[2]),
        pltpu.make_async_copy(eof_hbm, eof, local_sem.at[3]),
    ]
    for copy in copies:
        copy.start()
    levels = panel.shape[1] // count_z
    mine = pl.ds(pl.multiple_of(gz * levels, levels), levels)
    own_panel = pltpu.make_async_copy(
        panels_hbm.at[:, :, pl.ds(pl.multiple_of(gz * COLS, COLS), COLS)],
        panel.at[:, mine, :],
        local_sem.at[4],
    )
    own_panel.start()

    lane = lax.broadcasted_iota(jnp.int32, (8, COLS), 1)
    first_half = (lane & (SLOT - 1)) < HALF
    sub8 = lax.broadcasted_iota(jnp.int32, (8, COLS), 0)
    slots = [(lane >= SLOT * y) & (lane < SLOT * (y + 1)) for y in range(ROWS)]

    def slotted(edges, y, blocks):
        for g, block in enumerate(blocks):
            shifted = pltpu.roll(block, SLOT * y + HALF, 1)
            edges[g] = shifted if edges[g] is None else jnp.where(slots[y], shifted, edges[g])

    def pack_edges(edges, edge):
        for pair in range(0, len(edges), 2):
            one = edges[pair]
            two = edges[pair + 1] if pair + 1 < len(edges) else one
            easting = jnp.where(first_half, one, pltpu.roll(two, HALF, 1))
            westing = jnp.where(first_half, pltpu.roll(one, COLS - HALF, 1), two)
            edge[0, pair // 2] = easting.astype(jnp.bfloat16)
            edge[1, pair // 2] = westing.astype(jnp.bfloat16)

    members = panel.shape[0]
    sent_panels = []

    def send_panels(first, last, row, end):
        some = pl.ds(first, last - first)
        for d in range(1, count_z):
            peer = lax.rem(gz + d, count_z)
            spot = pl.ds(pl.multiple_of(gz * levels + row, 16), end - row)
            copy = pltpu.make_async_remote_copy(
                src_ref=panels_hbm.at[some, pl.ds(row, end - row), pl.ds(pl.multiple_of(peer * COLS, COLS), COLS)],
                dst_ref=panel.at[some, spot, :],
                send_sem=send_sem.at[33 + len(sent_panels)],
                recv_sem=recv_sem.at[33 + len(sent_panels)],
                device_id=peers[d - 1],
                device_id_type=MESH,
            )
            copy.start()
            sent_panels.append(copy)

    pl.semaphore_wait(barrier, len(partners))
    send_panels(0, 1, 0, 64)

    for copy in copies[:3]:
        copy.wait()
    edges = [None] * (GROUPS + 1)
    for y in range(ROWS):
        fields = control[pl.ds(y, PLANES, stride=ROWS), :]
        entries = coef_in[pl.ds(y, 8, stride=ROWS), :]
        high = entries.astype(jnp.bfloat16).astype(jnp.float32)
        blocks = [jnp.where(sub8 < 4, high, entries - high)]
        blocks += [fields[8 * g : 8 * g + 8] for g in range(GROUPS)]
        for g, block in enumerate(blocks[1:]):
            tile_a[g, y] = block.astype(jnp.bfloat16)
        if y % 2 == 0:
            even, even_high = entries, high
        else:
            both = jnp.where(sub8 < 4, even, entries)
            tile_c[1 + y // 2] = both.astype(jnp.bfloat16)
            if y in (1, ROWS - 1):
                left = both - jnp.where(sub8 < 4, even_high, high)
                tile_c[0 if y == 1 else 1 + ROWS // 2] = left.astype(jnp.bfloat16)
        slotted(edges, y, blocks)
    pack_edges(edges, edge_a)

    def exchange(first, chunks, tile, edge, north, south, side, extra=()):
        moves = [(edge.at[k % 2], side.at[k], sides[k]) for k in range(6)]
        moves += extra
        for a, b in chunks:
            groups = pl.ds(a, b - a)
            moves.append((tile.at[groups, pl.ds(ROWS - DEPTH, DEPTH)], south.at[groups], north_id))
            moves.append((tile.at[groups, pl.ds(0, DEPTH)], north.at[groups], south_id))
        return [
            pltpu.make_async_remote_copy(
                src_ref=source,
                dst_ref=target,
                send_sem=send_sem.at[first + k],
                recv_sem=recv_sem.at[first + k],
                device_id=device,
                device_id_type=MESH,
            )
            for k, (source, target, device) in enumerate(moves)
        ]

    extra = [
        (tile_c.at[pl.ds(1 + (ROWS - DEPTH) // 2, DEPTH // 2 + 1)], south_c, north_id),
        (tile_c.at[pl.ds(0, DEPTH // 2 + 1)], north_c, south_id),
    ]
    halo_a = exchange(0, CHUNKS_A, tile_a, edge_a, north_a, south_a, side_a, extra)
    for copy in halo_a:
        copy.start()
    send_panels(0, 1, 64, levels)
    send_panels(1, members, 0, levels)

    def put_coef(row, start, entries):
        for k in range(4):
            scale = TIME_STEP if k == 3 else 1.0
            entry = scale * entries[k : k + 1]
            coef[row, k, :, start : start + COLS] = jnp.broadcast_to(entry, (8, COLS))
            coef_rows[STRIDE * k + row : STRIDE * k + row + 1, start : start + COLS] = entry

    for y in range(ROWS):
        fields = control[pl.ds(y, PLANES, stride=ROWS), :]
        for g in range(GROUPS):
            grid[g, DEPTH + y, :, 0:COLS] = fields[8 * g : 8 * g + 8]
        put_coef(DEPTH + y, 0, coef_in[pl.ds(y, 8, stride=ROWS), :])

    turned[...] = jnp.zeros_like(turned)
    flux[...] = jnp.zeros_like(flux)
    for k in range(4):
        first = STRIDE * k + EXT
        coef_rows[first : STRIDE * (k + 1), :] = jnp.zeros((STRIDE - EXT, 2 * COLS), jnp.float32)
    coef_rows[4 * STRIDE :, :] = jnp.zeros((COLS - 4 * STRIDE, 2 * COLS), jnp.float32)

    copies[3].wait()
    count_e, count_f, count_l = eof.shape
    for e in range(count_e):
        block = eof[e].astype(jnp.float32)
        for f in range(count_f):
            basis[f * count_e + e : f * count_e + e + 1, :] = block[f : f + 1]
    plane = lax.broadcasted_iota(jnp.int32, (PLANES, 512), 0)
    field_of = jnp.zeros_like(plane)
    for f in range(1, count_f):
        field_of = field_of + jnp.where(plane >= f * count_e, 1, 0)
    spot = lax.broadcasted_iota(jnp.int32, (PLANES, 512), 1)
    same_field = field_of == (lax.shift_right_logical(spot, 5) & 3)
    level_row = lax.broadcasted_iota(jnp.int32, (count_l, 512), 0)
    level_spot = lax.broadcasted_iota(jnp.int32, (count_l, 512), 1)
    level_of = 4 * lax.shift_right_logical(level_spot, 7) + (lax.shift_right_logical(level_spot, 3) & 3)
    repeat = jnp.where(level_row == level_of, 1.0, 0.0).astype(jnp.bfloat16)
    spread = jnp.dot(basis[...].astype(jnp.bfloat16), repeat, preferred_element_type=jnp.float32)
    spread = jnp.where(same_field, spread, 0.0)
    for pair in range(ROWS // 2):
        both = [jnp.where((spot & 7) == 2 * pair + k, spread, 0.0) for k in range(2)]
        weight[pl.ds(2 * PLANES * pair, 2 * PLANES), :] = jnp.concatenate(both, axis=0).astype(jnp.bfloat16)

    keep_north = jnp.where(gy < count_y - 1, 1.0, 0.0).astype(jnp.float32)
    keep_south = jnp.where(gy > 0, 1.0, 0.0).astype(jnp.float32)
    ranges = (
        (DEPTH, 0, 0, ROWS, None),
        (0, 2, ROWS - DEPTH, DEPTH, keep_south),
        (DEPTH + ROWS, 4, 0, DEPTH, keep_north),
    )

    def edge_pack(side, group, k, keep):
        from_west = side[k, group // 2].astype(jnp.float32)
        from_east = side[k + 1, group // 2].astype(jnp.float32)
        if group % 2 == 0:
            pack = jnp.where(first_half, from_west, pltpu.roll(from_east, HALF, 1))
        else:
            pack = jnp.where(first_half, pltpu.roll(from_west, COLS - HALF, 1), from_east)
        return pack if keep is None else pack * keep

    def edge_rows(side, group):
        for start, k, slot, count, keep in ranges:
            pack = edge_pack(side, group, k, keep)
            for y in range(count):
                yield start + y, pltpu.roll(pack, COLS - HALF - SLOT * (y + slot), 1)

    def halo_rows(north, south, group):
        for y in range(DEPTH):
            yield y, south[group, y].astype(jnp.float32) * keep_south
            yield DEPTH + ROWS + y, north[group, y].astype(jnp.float32) * keep_north

    def joined(parts):
        return parts + pltpu.roll(parts, 4, 0)

    for copy in halo_a[:8]:
        copy.wait_recv()
    for row, block in edge_rows(side_a, 0):
        put_coef(row, COLS, joined(block))
    for half in range(DEPTH // 2):
        lower = south_c[half].astype(jnp.float32)
        upper = north_c[1 + half].astype(jnp.float32)
        if half == DEPTH // 2 - 1:
            lower = lower + south_c[half + 1].astype(jnp.float32)
        if half == 0:
            upper = upper + north_c[0].astype(jnp.float32)
        lower, upper = lower * keep_south, upper * keep_north
        for k in range(2):
            put_coef(2 * half + k, 0, lower[4 * k : 4 * k + 4])
            put_coef(DEPTH + ROWS + 2 * half + k, 0, upper[4 * k : 4 * k + 4])
    for g in range(GROUPS):
        for row, block in edge_rows(side_a, g + 1):
            grid[g, row, :, COLS:] = block
    for i, (a, b) in enumerate(CHUNKS_A):
        for copy in halo_a[8 + 2 * i : 10 + 2 * i]:
            copy.wait_recv()
        for g in range(a, b):
            for row, block in halo_rows(north_a, south_a, g):
                grid[g, row, :, 0:COLS] = block

        def step_a(g, carry):
            adjoint_steps(grid, coef, g)
            return carry

        lax.fori_loop(a, b, step_a, 0)


    pick_row = lax.broadcasted_iota(jnp.int32, (COLS, LINES * COLS), 0)
    pick_lane = lax.broadcasted_iota(jnp.int32, (COLS, LINES * COLS), 1)
    line_of = lax.shift_right_logical(pick_lane, 7)
    pick_lane = pick_lane & (COLS - 1)
    block_of = jnp.where(pick_lane >= PLANES, 1, 0) + jnp.where(pick_lane >= 2 * PLANES, 1, 0)
    wanted = jnp.where(pick_lane < 3 * PLANES, line_of + LINES * block_of, 2 * COLS)
    own, beyond = coef_rows[:, 0:COLS].T, coef_rows[:, COLS:].T
    rest = jnp.concatenate([beyond[COLS - 8 :], own, beyond[0:8]], axis=0)
    parts = []
    for _ in range(3):
        parts.append(rest.astype(jnp.bfloat16))
        rest = rest - parts[-1].astype(jnp.float32)
    left = jnp.concatenate(parts, axis=1)
    for k in range(4):
        ones = jnp.where(pick_row - STRIDE * k == wanted, 1.0, 0.0).astype(jnp.bfloat16)
        turn = jnp.dot(left, jnp.concatenate([ones] * 3, axis=0), preferred_element_type=jnp.float32)
        for g in range(LINES):
            coef_t[k, g] = turn[:, g * COLS : (g + 1) * COLS]

    own_panel.wait()
    for copy in sent_panels:
        copy.wait_recv()
    for m in range(0, members, 2):
        pair = jnp.concatenate([panel[m], panel[m + 1]], axis=1)
        projected[:, m * COLS : (m + 2) * COLS] = jnp.dot(
            weight[...], pair, preferred_element_type=jnp.float32
        )

    edges = [None] * GROUPS
    for y in range(ROWS):
        factor = jnp.concatenate([grid[g, DEPTH + y, :, 0:COLS] for g in range(GROUPS)], axis=0)
        row = None
        for m in range(members):
            term = projected[y * PLANES : (y + 1) * PLANES, m * COLS : (m + 1) * COLS]
            score = jnp.sum(term * factor, axis=0, keepdims=True) * (1.0 / (members - 1))
            row = term * score if row is None else row + term * score
        blocks = [row[8 * g : 8 * g + 8] for g in range(GROUPS)]
        for g, block in enumerate(blocks):
            own_b[g, y] = block
            tile_b[g, y] = block.astype(jnp.bfloat16)
        slotted(edges, y, blocks)
    pack_edges(edges, edge_b)

    first_b = len(halo_a)
    halo_b = exchange(first_b, CHUNKS_B, tile_b, edge_b, north_b, south_b, side_b)
    for copy in halo_b:
        copy.start()
    for copy in halo_b[:6]:
        copy.wait_recv()
    lanes = lax.broadcasted_iota(jnp.int32, (8, COLS), 1)
    spare = jnp.zeros((COLS - 3 * PLANES, COLS), jnp.float32)
    packs = [edge_pack(side_b, g, k, keep) for k, keep in ((2, keep_south), (0, None), (4, keep_north)) for g in range(GROUPS)]
    packs = jnp.concatenate(packs + [spare], axis=0).T
    for east_side in range(2):
        place_at = pl.ds(east_side * (TALL - 8), 8)

        def piece(y):
            first = SLOT * y + HALF * east_side
            return packs[first : first + 8]

        for g in range(DEPTH):
            middle = jnp.where(lanes < 2 * PLANES, piece(1 + g), piece(g))
            turned[g, place_at] = jnp.where(lanes < PLANES, piece(2 + g), middle)
        turned[DEPTH, place_at] = jnp.where(lanes < PLANES, pltpu.roll(piece(0), COLS - PLANES, 1), piece(ROWS - 1))
    main = pl.ds(8, COLS)
    ends = [own_b[g, y] for y in (0, ROWS - 1) for g in range(GROUPS)]
    ends.append(jnp.zeros((COLS - 2 * PLANES, COLS), jnp.float32))
    turned[DEPTH, main] = jnp.concatenate(ends, axis=0).T
    for copy in halo_b[6:]:
        copy.wait_recv()
    for line in range(DEPTH):
        stack = [south_b[g, line].astype(jnp.float32) * keep_south for g in range(GROUPS)]
        stack += [own_b[g, 1 + line] for g in range(GROUPS)]
        stack += [north_b[g, line].astype(jnp.float32) * keep_north for g in range(GROUPS)]
        turned[line, main] = jnp.concatenate(stack + [spare], axis=0).T
    forward_steps(turned, flux, coef_t)
    stores = []

    def store(y, block):
        finished[y] = block
        stores.append(pltpu.make_async_copy(finished.at[y], out_ref.at[:, y, :], local_sem.at[5 + y]))
        stores[-1].start()

    for line in range(LINES):
        back = turned[line, main].T
        if line < DEPTH:
            store(1 + line, back[PLANES : 2 * PLANES])
        else:
            store(0, back[0:PLANES])
            store(ROWS - 1, back[PLANES : 2 * PLANES])
    for copy in halo_a + sent_panels + halo_b:
        copy.wait_send()
    for copy in stores:
        copy.wait()


def solution(mesh):
    sizes = tuple(mesh.shape[name] for name in ("gx", "gy", "gz"))

    def per_device(panels, eof_basis, control, coefficients):
        members, fields, levels, rows, columns = panels.shape
        eof_count = eof_basis.shape[2]
        deep = fields * levels * rows
        f32, bf16 = jnp.float32, jnp.bfloat16
        anywhere = pl.BlockSpec(memory_space=pl.ANY)
        wide = GROUPS + 1
        pairs_a, pairs_b = wide // 2, (GROUPS + 1) // 2
        out = pl.pallas_call(
            functools.partial(kernel, sizes),
            out_shape=jax.ShapeDtypeStruct((PLANES, ROWS, COLS), f32),
            in_specs=[anywhere] * 4,
            out_specs=anywhere,
            scratch_shapes=[
                pltpu.VMEM((PLANES * ROWS, COLS), f32),
                pltpu.VMEM((8 * ROWS, COLS), f32),
                pltpu.VMEM((eof_count, fields, levels * sizes[2]), bf16),
                pltpu.VMEM((PLANES, levels * sizes[2]), f32),
                pltpu.VMEM((members, deep * sizes[2], COLS), bf16),
                pltpu.VMEM((PLANES * ROWS, deep * sizes[2]), bf16),
                pltpu.VMEM((PLANES * ROWS, members * COLS), f32),
                pltpu.VMEM((GROUPS, EXT, 8, 2 * COLS), f32),
                pltpu.VMEM((EXT, 4, 8, 2 * COLS), f32),
                pltpu.VMEM((ROWS // 2 + 2, 8, COLS), bf16),
                pltpu.VMEM((DEPTH // 2 + 1, 8, COLS), bf16),
                pltpu.VMEM((DEPTH // 2 + 1, 8, COLS), bf16),
                pltpu.VMEM((GROUPS, ROWS, 8, COLS), bf16),
                pltpu.VMEM((2, pairs_a, 8, COLS), bf16),
                pltpu.VMEM((GROUPS, DEPTH, 8, COLS), bf16),
                pltpu.VMEM((GROUPS, DEPTH, 8, COLS), bf16),
                pltpu.VMEM((6, pairs_a, 8, COLS), bf16),
                pltpu.VMEM((GROUPS, ROWS, 8, COLS), bf16),
                pltpu.VMEM((2, pairs_b, 8, COLS), bf16),
                pltpu.VMEM((GROUPS, DEPTH, 8, COLS), bf16),
                pltpu.VMEM((GROUPS, DEPTH, 8, COLS), bf16),
                pltpu.VMEM((6, pairs_b, 8, COLS), bf16),
                pltpu.VMEM((GROUPS, ROWS, 8, COLS), f32),
                pltpu.VMEM((LINES, TALL + 8, COLS), f32),
                pltpu.VMEM((LINES, TALL + 8, COLS), f32),
                pltpu.VMEM((COLS, 2 * COLS), f32),
                pltpu.VMEM((4, LINES, TALL, COLS), f32),
                pltpu.VMEM((ROWS, PLANES, COLS), f32),
                pltpu.SemaphoreType.DMA((5 + ROWS,)),
                pltpu.SemaphoreType.DMA((44,)),
                pltpu.SemaphoreType.DMA((44,)),
            ],
            compiler_params=pltpu.CompilerParams(
                collective_id=0, has_side_effects=True, vmem_limit_bytes=63 * 1024 * 1024
            ),
            name="covariance",
        )(
            panels.reshape(members, deep, columns),
            eof_basis.transpose(2, 0, 1),
            control.reshape(-1, COLS),
            coefficients.reshape(-1, COLS),
        )
        return out.reshape(control.shape)

    in_specs = (
        P(None, None, "gz", "gy", "gx"),
        P(),
        P(None, None, "gy", ("gx", "gz")),
        P(None, "gy", ("gx", "gz")),
    )
    return jax.shard_map(
        per_device,
        mesh=mesh,
        in_specs=in_specs,
        out_specs=P(None, None, "gy", ("gx", "gz")),
        check_vma=False,
    )
```
